128 devices in a mesh: rows: 32 (over x, z, core), feat: 4 (over y).
Axes of the slice: x: 4, y: 4, z: 4, core: 2. Of those that a mesh axis runs over, the one named last changes fastest.
Arguments:
- binned: int32 [65536, 256], P('rows', 'feat'), may hold values from 0 to 255
- node_index: int32 [65536, 1], P('rows'), may hold values from 0 to 31; in each aligned block of 2048 rows (0 to 2047, 2048 to 4095, ...) at most 128 rows name the same one
- treatment: float32 [65536], P('rows'), may hold values from -6 to 6
- outcome: float32 [65536], P('rows'), may hold values from -6 to 6
- unit_weight: float32 [65536], P('rows'), may hold values from 0.1 to 2
- root_feature: int32 [32], replicated, may hold values from 0 to 255
- root_cutoff: int32 [32], replicated, may hold values from 64 to 191
- child_feature: int32 [64], replicated, may hold values from 0 to 255
- child_cutoff: int32 [64], replicated, may hold values from 64 to 191
Outputs:
- node_moments: float32 [32, 3, 256, 256], P('rows', None, 'feat')
- child_moments: float32 [64, 3, 256, 256], P('rows', None, 'feat')
- leaf_moments: float32 [128, 3, 256, 256], P('rows', None, 'feat')
The draws below stay inside these ranges and needn't reach their ends.
Inputs may be any that keep to these rules, and one draw needn't show every extreme that they name: `node_index`: among the rows of one device no node is named by more than 128 rows, a bound that some block reaches.
All inputs are finite; a program needn't handle non-finite values.
Results may differ from the reference program's by a relative error of at most 0.0022.
Values may be sent and summed in bfloat16 or wider, within the bound.
No kernel may reach another device: no remote copies, remote signals or barrier semaphores. Data moves between devices by JAX's collectives and lax.ppermute only.
A program may use at most 64 MiB of HBM per device.

```python
import math
import jax
import jax.numpy as jnp
import numpy as np
from jax import lax

FEATURES = 256
BINS = 256
ROW_DEV = 2048
ROWS = 65536
NODES = 32
CAPACITY = 128


def touch_ends(entries, rng, least, top_value):
    dims = entries.shape
    spot = [jax.random.randint(jax.random.fold_in(rng, axis), (), 0, dims[axis]) for axis in range(len(dims))]
    entries = entries.at[tuple(spot)].set(least)
    longest = dims.index(max(dims))
    spot[longest] = (spot[longest] + 1) % dims[longest]
    return entries.at[tuple(spot)].set(top_value)


def levels(own_key, shape, cuts, least, top_value):
    factor_of, own = 1.0, jax.random.fold_in(own_key, 6)
    for position, parts in cuts:
        steps = jnp.exp(jax.random.uniform(jax.random.fold_in(own, position), (parts,), jnp.float32, least / len(cuts), top_value / len(cuts)))
        factor_of = factor_of * jnp.repeat(steps, shape[position] // parts).reshape([-1 if axis == position else 1 for axis in range(len(shape))])
    return factor_of


def shared_out(rng, own, number, rows, number_of, top, limit, slope):
    order = jax.random.permutation(rng, number_of)
    packed, common = shares(number_of, rows * top, limit, slope, True), shares(number_of, rows * top, limit, slope, False)
    places = jnp.arange(number_of)

    def named(sizes, offset_by):
        used = int((sizes > 0).sum())
        fixed = max(1, used // 4)
        shifted = fixed + (places - fixed + offset_by * (used - fixed)) % max(1, number_of - fixed)
        return jnp.zeros((number_of,), jnp.int32).at[order[jnp.where(places < fixed, places, shifted)]].set(jnp.asarray(sizes, jnp.int32))

    sizes = jnp.where(number % 4 == 0, named(packed, number // 4), named(common, number - number // 4 - 1))
    mixed = jax.random.permutation(jax.random.fold_in(own, 3), number_of)
    donor, taker = mixed[0:number_of // 2 * 2:2], mixed[1:number_of // 2 * 2:2]
    slack = jnp.minimum(sizes[donor] - 1, limit - sizes[taker]) // 2
    slack = jnp.where((donor == order[0]) | (taker == order[0]) | (sizes[taker] == 0), 0, jnp.maximum(slack, 0))
    shifted = jax.random.randint(jax.random.fold_in(own, 4), (number_of // 2,), 0, 1 << 20) % (slack + 1)
    sizes = sizes.at[donor].add(-shifted).at[taker].add(shifted)
    members = jnp.searchsorted(jnp.cumsum(sizes), jnp.arange(rows * top), side="right").astype(jnp.int32)
    listing = members.reshape(top, rows).T
    listing = listing[jax.random.permutation(jax.random.fold_in(own, 1), rows)]
    offset_by = jax.random.randint(jax.random.fold_in(own, 2), (rows, 1), 0, top)
    return jnp.take_along_axis(listing, (jnp.arange(top)[None, :] + offset_by) % top, axis=1)


def shares(count, total, most, lean, full):
    loads = [(1 << 20) // math.isqrt(grade ** lean) + 1 for grade in range(1, count + 1)]
    largest = most if full else min(most, max(-(-total // count), total * loads[0] // sum(loads)))
    least = 1 if total - largest >= count - 1 else 0
    holding, spare = [largest] + [least] * (count - 1), total - largest - least * (count - 1)
    while spare > 0:
        free = [i for i in range(1, count) if holding[i] < largest] or [i for i in range(1, count) if holding[i] < most]
        pool, budget = sum([loads[i] for i in free]), spare
        for i in free:
            addition = min(most - holding[i], max(1, budget * loads[i] // pool), spare)
            holding[i] = holding[i] + addition
            spare = spare - addition
    return np.array(holding)


def centred(stream_key, shape, spread, bound, pieces=(), kind=jnp.bfloat16):
    loudness = levels(stream_key, shape, pieces, -0.22, 0.18) if pieces else 1.0
    drawn = jax.random.normal(stream_key, shape, jnp.float32) * spread * loudness
    return jnp.minimum(jnp.maximum(drawn, -bound), bound).astype(kind)


def setup_inputs(seed: int = 0) -> dict:
    key_list = jax.random.split(jax.random.key(seed), 10)
    binned = touch_ends(jax.random.randint(key_list[0], (ROWS, FEATURES), 0, BINS), jax.random.fold_in(key_list[0], 1), 0, BINS - 1).astype(jnp.int32)
    node_index_keys = jax.random.split(jax.random.fold_in(key_list[1], 1), ROWS // ROW_DEV)
    node_index_turns = jax.random.permutation(jax.random.fold_in(key_list[1], 3), ROWS // ROW_DEV)
    node_index = jax.vmap(lambda own, number: shared_out(jax.random.fold_in(key_list[1], 2), own, number, ROW_DEV, NODES, 1, CAPACITY, 1))(node_index_keys, node_index_turns).reshape((ROWS, 1))
    treatment = centred(key_list[2], (ROWS,), 1.0, 6.0, ((0, 32),), jnp.float32)
    outcome = centred(key_list[3], (ROWS,), 1.0, 6.0, ((0, 32),), jnp.float32)
    unit_weight = jnp.clip(jnp.exp(math.log(2.0) - 2.9957323 * jax.random.uniform(key_list[4], (ROWS,), jnp.float32) ** levels(key_list[4], (ROWS,), ((0, 32),), -0.2, 0.2)), 0.1, 2.0)
    root_feature = touch_ends(jax.random.randint(key_list[5], (NODES,), 0, FEATURES), jax.random.fold_in(key_list[5], 1), 0, FEATURES - 1).astype(jnp.int32)
    root_cutoff = touch_ends(jax.random.randint(key_list[6], (NODES,), BINS // 4, 3 * BINS // 4), jax.random.fold_in(key_list[6], 1), BINS // 4, (3 * BINS // 4) - 1).astype(jnp.int32)
    child_feature = touch_ends(jax.random.randint(key_list[7], (2 * NODES,), 0, FEATURES), jax.random.fold_in(key_list[7], 1), 0, FEATURES - 1).astype(jnp.int32)
    child_cutoff = touch_ends(jax.random.randint(key_list[8], (2 * NODES,), BINS // 4, 3 * BINS // 4), jax.random.fold_in(key_list[8], 1), BINS // 4, (3 * BINS // 4) - 1).astype(jnp.int32)
    return {"binned": binned, "node_index": node_index, "treatment": treatment, "outcome": outcome, "unit_weight": unit_weight, "root_feature": root_feature, "root_cutoff": root_cutoff, "child_feature": child_feature, "child_cutoff": child_cutoff}


def reference(binned, node_index, treatment, outcome, unit_weight, root_feature, root_cutoff, child_feature, child_cutoff):
    tree_node = node_index[:, 0]
    rounded = jnp.stack([unit_weight, unit_weight * treatment * treatment, unit_weight * treatment * outcome], 1).astype(jnp.bfloat16)
    moments = lax.optimization_barrier(rounded).astype(jnp.float32)
    positions = jnp.arange(ROWS, dtype=jnp.int32)
    root_bins = binned[positions, root_feature[tree_node]]
    right_root = (root_bins > root_cutoff[tree_node]).astype(jnp.int32)
    child_index = (2 * tree_node + right_root).astype(jnp.int32)
    child_bins = binned[positions, child_feature[child_index]]
    right_child = (child_bins > child_cutoff[child_index]).astype(jnp.int32)
    leaf_index = (2 * child_index + right_child).astype(jnp.int32)

    def per_feature(column):
        segment_ids = (leaf_index * BINS + column).astype(jnp.int32)
        return jax.ops.segment_sum(moments, segment_ids, num_segments=4 * NODES * BINS)

    totals = lax.map(per_feature, binned.T)
    leaf_moments = totals.reshape(FEATURES, 4 * NODES, BINS, 3).transpose(1, 3, 0, 2)
    child_moments = leaf_moments.reshape(2 * NODES, 2, 3, FEATURES, BINS).sum(1)
    node_moments = leaf_moments.reshape(NODES, 4, 3, FEATURES, BINS).sum(1)
    return node_moments, child_moments, leaf_moments
```

```python
import jax
import jax.numpy as jnp
from jax import lax
from jax.experimental import pallas as pl
from jax.experimental.pallas import tpu as pltpu
from jax.sharding import PartitionSpec as P

BINS = 256
BF = jnp.bfloat16
F32 = jnp.float32
NT = (((1,), (1,)), ((), ()))
NN = (((1,), (0,)), ((), ()))


def iota(shape, axis):
    return lax.broadcasted_iota(jnp.int32, shape, axis)


def split_kernel(where_ref, bins_ref, node_ref, rf_ref, rc_ref, cf_ref, cc_ref, bits_ref):
    feats, rows = bins_ref.shape
    nodes = rf_ref.shape[1]
    first = where_ref[0] * feats
    bins = bins_ref[...].astype(F32)
    node = node_ref[...]

    def decide(feature_row, cutoff_row, index, count):
        here = (feature_row - first == iota((feats, count), 0)).astype(F32)
        table = jnp.concatenate([here, jnp.broadcast_to(cutoff_row.astype(F32), (8, count))], 0)
        hot = (iota((count, rows), 0) == index).astype(F32).astype(BF)
        got = lax.dot_general(table.astype(BF), hot, NN, preferred_element_type=F32)
        right = jnp.where(bins > got[feats : feats + 1], got[:feats], 0.0)
        return jnp.sum(right, 0, keepdims=True)

    root = decide(rf_ref[...], rc_ref[...], node, nodes)
    left = decide(cf_ref[...], cc_ref[...], 2 * node, 2 * nodes)
    right = decide(cf_ref[...], cc_ref[...], 2 * node + 1, 2 * nodes)
    bits_ref[...] = jnp.concatenate([root, left, right, jnp.zeros((5, rows), F32)], 0).astype(BF)


def place_kernel(bins_ref, node_ref, out_ref, code_ref, a_ref):
    feats, rows = bins_ref.shape
    nodes, _, cap = out_ref.shape
    blocks = rows // 256
    node = node_ref[...]
    hot = (iota((nodes, rows), 0) == node).astype(F32)
    stacked = jnp.concatenate([hot[:, b * 256 : (b + 1) * 256] for b in range(blocks)], 0)
    before = (iota((256, 256), 0) < iota((256, 256), 1)).astype(F32).astype(BF)
    ones = jnp.ones((256, 256), BF)
    inner = lax.dot_general(stacked.astype(BF), before, NN, preferred_element_type=F32)
    total = lax.dot_general(stacked.astype(BF), ones, NN, preferred_element_type=F32)
    carry = jnp.zeros((nodes, 256), F32)
    ranks = []
    for b in range(blocks):
        part = slice(b * nodes, (b + 1) * nodes)
        ranks.append(jnp.sum(stacked[part] * (inner[part] + carry), 0, keepdims=True))
        carry = carry + total[part]
    rank = jnp.concatenate(ranks, 1)
    code = rank + (node % 2 * cap).astype(F32)
    code_ref[...] = code
    slot_hot = (iota((2 * cap, rows), 0) == code.astype(jnp.int32)).astype(F32).astype(BF)
    bins = bins_ref[...].astype(F32).astype(BF)
    pair = jnp.broadcast_to(node // 2, (feats, rows))
    for p in range(nodes // 2):
        a_ref[p * feats : (p + 1) * feats, :] = jnp.where(pair == p, bins, jnp.zeros((), BF))
    moved = lax.dot_general(a_ref[...], slot_hot, NT, preferred_element_type=F32).astype(BF)
    for p in range(nodes // 2):
        piece = moved[p * feats : (p + 1) * feats]
        out_ref[2 * p, :feats, :] = piece[:, :cap]
        out_ref[2 * p + 1, :feats, :] = piece[:, cap:]


def value_kernel(
    b0_ref, b1_ref, b2_ref, b3_ref, node_ref, code_ref, w_ref, t_ref, y_ref, buf_ref, out_ref,
    part_ref, sem,
):
    nodes, _, cap = part_ref.shape
    rows = node_ref.shape[1]
    bits = (b0_ref[...].astype(F32) + b1_ref[...].astype(F32)) + (
        b2_ref[...].astype(F32) + b3_ref[...].astype(F32)
    )
    root = bits[0:1]
    leaf = 2.0 * root + jnp.where(root > 0.5, bits[2:3], bits[1:2])
    w = w_ref[...]
    t = t_ref[...]
    y = y_ref[...]
    carried = jnp.concatenate(
        [w, w * t * t, w * t * y, leaf, jnp.zeros((4, rows), F32)], 0
    )
    node = node_ref[...]
    slot_hot = (iota((2 * cap, rows), 0) == code_ref[...].astype(jnp.int32)).astype(F32).astype(BF)
    pair = jnp.broadcast_to(node // 2, (8, rows))
    spread = jnp.concatenate(
        [jnp.where(pair == p, carried, 0.0) for p in range(nodes // 2)], 0
    ).astype(BF)
    moved = lax.dot_general(spread, slot_hot, NT, preferred_element_type=F32).astype(BF)
    for p in range(nodes // 2):
        piece = moved[p * 8 : (p + 1) * 8]
        part_ref[2 * p] = piece[:, :cap]
        part_ref[2 * p + 1] = piece[:, cap:]
    copy = pltpu.make_async_copy(part_ref, out_ref.at[:, pl.ds(out_ref.shape[1] - 8, 8), :], sem)
    copy.start()
    copy.wait()


HI = 4
LO = BINS // HI


def hist_kernel(
    got_ref, node_ref, child_ref, leaf_ref, hi_ref, lo_ref, w_ref, half0_ref, half1_ref
):
    halves = (half0_ref, half1_ref)
    sources, depth, cap = got_ref.shape
    feats = depth - 8
    cols = leaf_ref.shape[0] // feats
    slots = sources * cap
    for s in range(sources):
        at = slice(s * cap, (s + 1) * cap)
        x = got_ref[s, :feats, :].astype(F32)
        hi = jnp.floor(x * (1.0 / LO))
        hi_ref[:, at] = hi
        lo_ref[:, at] = x - hi * LO
        tail = got_ref[s, feats:, :].astype(F32)
        position = jnp.broadcast_to(tail[3:4], (3, cap))
        columns = jnp.concatenate(
            [jnp.where(position == float(q), tail[:3], 0.0) for q in range(cols // 3)], 0
        )
        w_ref[:, at] = jnp.concatenate([columns] * HI, 0).astype(BF)
    hi_of = (iota((HI * cols, slots), 0) // cols).astype(F32).astype(BF)
    lo_of = iota((LO, slots), 0).astype(F32).astype(BF)
    one = jnp.ones((), BF)
    zero = jnp.zeros((), BF)

    def step(f, carry):
        hi = jnp.broadcast_to(hi_ref[pl.ds(f, 1), :], (HI * cols, slots)).astype(BF)
        lo = jnp.broadcast_to(lo_ref[pl.ds(f, 1), :], (LO, slots)).astype(BF)
        a = jnp.where(hi == hi_of, w_ref[...], zero)
        b = jnp.where(lo == lo_of, one, zero)
        res = lax.dot_general(a, b, NT, preferred_element_type=F32)
        for half in range(2):
            parts = [res[h * cols : (h + 1) * cols] for h in (2 * half, 2 * half + 1)]
            halves[half][pl.ds(f, cols, stride=feats), :] = jnp.concatenate(parts, 1)
        return carry

    lax.fori_loop(0, feats, step, 0)
    size = 3 * feats
    leaf_ref[:, : BINS // 2] = half0_ref[...]
    leaf_ref[:, BINS // 2 :] = half1_ref[...]
    for c in range(cols // 6):
        child_ref[c * size : (c + 1) * size, :] = (
            leaf_ref[2 * c * size : (2 * c + 1) * size, :]
            + leaf_ref[(2 * c + 1) * size : (2 * c + 2) * size, :]
        )
    node_ref[...] = child_ref[:size, :] + child_ref[size:, :]


def vmem(n):
    return [pl.BlockSpec(memory_space=pltpu.VMEM)] * n


def on_device(
    binned,
    node_index,
    treatment,
    outcome,
    unit_weight,
    root_feature,
    root_cutoff,
    child_feature,
    child_cutoff,
):
    rows, feats = binned.shape
    nodes = root_feature.shape[0]
    owners = lax.axis_size("rows")
    feat_devices = lax.axis_size("feat")
    cap = 2 * rows // nodes
    depth = feats + 8
    params = pltpu.CompilerParams(vmem_limit_bytes=48 << 20)
    bins = binned.T
    node = node_index.T
    where = lax.axis_index("feat").astype(jnp.int32)[None]
    own = pl.pallas_call(
        split_kernel,
        out_shape=jax.ShapeDtypeStruct((8, rows), BF),
        in_specs=[pl.BlockSpec(memory_space=pltpu.SMEM)] + vmem(6),
        out_specs=vmem(1)[0],
        compiler_params=params,
        name="split",
    )(where, bins, node, root_feature[None], root_cutoff[None], child_feature[None], child_cutoff[None])
    others = [
        lax.ppermute(own, "feat", [(i, (i + k) % feat_devices) for i in range(feat_devices)])
        for k in range(1, feat_devices)
    ]
    buf, code = pl.pallas_call(
        place_kernel,
        out_shape=[
            jax.ShapeDtypeStruct((nodes, depth, cap), BF),
            jax.ShapeDtypeStruct((1, rows), F32),
        ],
        in_specs=vmem(2),
        out_specs=vmem(2),
        scratch_shapes=[pltpu.VMEM((nodes // 2 * feats, rows), BF)],
        compiler_params=params,
        name="place",
    )(bins, node)
    buf = pl.pallas_call(
        value_kernel,
        out_shape=jax.ShapeDtypeStruct((nodes, depth, cap), BF),
        in_specs=vmem(9) + [pl.BlockSpec(memory_space=pl.ANY)],
        out_specs=pl.BlockSpec(memory_space=pl.ANY),
        scratch_shapes=[pltpu.VMEM((nodes, 8, cap), BF), pltpu.SemaphoreType.DMA],
        input_output_aliases={9: 0},
        compiler_params=params,
        name="value",
    )(own, *others, node, code, unit_weight[None], treatment[None], outcome[None], buf)
    got = lax.all_to_all(buf, "rows", 0, 0, tiled=True)
    shape = lambda n: jax.ShapeDtypeStruct((n * 3 * feats, BINS), F32)
    node_moments, child_moments, leaf_moments = pl.pallas_call(
        hist_kernel,
        out_shape=[shape(1), shape(2), shape(4)],
        in_specs=vmem(1),
        out_specs=vmem(3),
        scratch_shapes=[
            pltpu.VMEM((feats, owners * cap), F32),
            pltpu.VMEM((feats, owners * cap), F32),
            pltpu.VMEM((HI * 12, owners * cap), BF),
            pltpu.VMEM((12 * feats, BINS // 2), F32),
            pltpu.VMEM((12 * feats, BINS // 2), F32),
        ],
        compiler_params=params,
        name="hist",
    )(got)
    return (
        node_moments.reshape(1, 3, feats, BINS),
        child_moments.reshape(2, 3, feats, BINS),
        leaf_moments.reshape(4, 3, feats, BINS),
    )


def solution(mesh):
    in_specs = (
        P("rows", "feat"),
        P("rows", None),
        P("rows"),
        P("rows"),
        P("rows"),
        P(),
        P(),
        P(),
        P(),
    )
    out_specs = (
        P("rows", None, "feat", None),
        P("rows", None, "feat", None),
        P("rows", None, "feat", None),
    )
    return jax.shard_map(
        on_device, mesh=mesh, in_specs=in_specs, out_specs=out_specs, check_vma=False
    )
```

```python
import jax
import jax.numpy as jnp
from jax import lax
from jax.experimental import pallas as pl
from jax.experimental.pallas import tpu as pltpu
from jax.sharding import PartitionSpec as P

BINS = 256
BF = jnp.bfloat16
F32 = jnp.float32
NT = (((1,), (1,)), ((), ()))
NN = (((1,), (0,)), ((), ()))
HI = 4
LO = BINS // HI


def iota(shape, axis):
    return lax.broadcasted_iota(jnp.int32, shape, axis)


def place_kernel(
    owner_ref, place_ref, rf_ref, rc_ref, cf_ref, cc_ref, bins_hbm, node_hbm, w_hbm, t_hbm, y_hbm,
    out_ref, split_ref, bins_ref, node_ref, w_ref, t_ref, y_ref, a_ref, sems,
):
    copies = [
        pltpu.make_async_copy(source, target, sems.at[i])
        for i, (source, target) in enumerate(
            zip((node_hbm, w_hbm, t_hbm, y_hbm, bins_hbm), (node_ref, w_ref, t_ref, y_ref, bins_ref))
        )
    ]
    for copy in copies:
        copy.start()
    feats, rows = bins_ref.shape
    nodes, depth, cap = out_ref.shape
    blocks = rows // 256
    own = owner_ref[0]
    first = place_ref[0] * feats
    table = [
        rf_ref[own] - first, cf_ref[2 * own] - first, cf_ref[2 * own + 1] - first,
        rc_ref[own], cc_ref[2 * own], cc_ref[2 * own + 1],
    ]
    for k, entry in enumerate(table):
        split_ref[k : k + 1, :] = jnp.full((1, cap), entry, jnp.int32)
    copies[0].wait()
    node = node_ref[...]
    hot = (iota((nodes, rows), 0) == node).astype(F32)
    stacked = jnp.concatenate([hot[:, b * 256 : (b + 1) * 256] for b in range(blocks)], 0)
    before = (iota((256, 256), 0) < iota((256, 256), 1)).astype(F32).astype(BF)
    ones = jnp.ones((256, 256), BF)
    inner = lax.dot_general(stacked.astype(BF), before, NN, preferred_element_type=F32)
    total = lax.dot_general(stacked.astype(BF), ones, NN, preferred_element_type=F32)
    carry = jnp.zeros((nodes, 256), F32)
    ranks = []
    for b in range(blocks):
        part = slice(b * nodes, (b + 1) * nodes)
        ranks.append(jnp.sum(stacked[part] * (inner[part] + carry), 0, keepdims=True))
        carry = carry + total[part]
    rank = jnp.concatenate(ranks, 1)
    code = rank.astype(jnp.int32) + node % 2 * cap
    slot_hot = (iota((2 * cap, rows), 0) == code).astype(F32).astype(BF)
    for copy in copies[1:4]:
        copy.wait()
    w = w_ref[...]
    t = t_ref[...]
    y = y_ref[...]
    carried = jnp.concatenate([w, w * t * t, w * t * y, jnp.zeros((depth - feats - 3, rows), F32)], 0)
    copies[4].wait()
    bins = jnp.concatenate([bins_ref[...].astype(F32), carried], 0).astype(BF)
    pair = jnp.broadcast_to(node // 2, (depth, rows))
    for p in range(nodes // 2):
        a_ref[p * depth : (p + 1) * depth, :] = jnp.where(pair == p, bins, jnp.zeros((), BF))
    moved = lax.dot_general(a_ref[...], slot_hot, NT, preferred_element_type=F32).astype(BF)
    for p in range(nodes // 2):
        piece = moved[p * depth : (p + 1) * depth]
        out_ref[2 * p] = piece[:, :cap]
        out_ref[2 * p + 1] = piece[:, cap:]


def split_kernel(split_ref, got_ref, bits_ref):
    sources, depth, cap = got_ref.shape
    feats = depth - 8
    feature = iota((feats, cap), 0)
    masks = [feature == split_ref[k : k + 1, :] for k in range(3)]
    cutoffs = [split_ref[k : k + 1, :].astype(F32) for k in range(3, 6)]
    rows = [[], [], []]
    for s in range(sources):
        x = got_ref[s, :feats, :].astype(F32)
        for k in range(3):
            right = jnp.where(jnp.logical_and(masks[k], x > cutoffs[k]), 1.0, 0.0)
            rows[k].append(jnp.sum(right, 0, keepdims=True))
    for k in range(3):
        bits_ref[k] = jnp.concatenate(rows[k], 0).astype(BF)


def hist_kernel(
    got_ref, b0_ref, b1_ref, b2_ref, b3_ref, node_ref, child_ref, leaf_ref, hi_ref, lo_ref, w_ref,
    half0_ref, half1_ref,
):
    sources, depth, cap = got_ref.shape
    feats = depth - 8
    cols = leaf_ref.shape[0] // feats
    halves = (half0_ref, half1_ref)
    bits = (b0_ref[...].astype(F32) + b1_ref[...].astype(F32)) + (
        b2_ref[...].astype(F32) + b3_ref[...].astype(F32)
    )
    leaf = 2.0 * bits[0] + jnp.where(bits[0] > 0.5, bits[2], bits[1])
    for s in range(sources):
        x = got_ref[s, :feats, :].astype(F32)
        hi = jnp.floor(x * (1.0 / LO))
        hi_ref[s * feats : (s + 1) * feats, :] = hi
        lo_ref[s * feats : (s + 1) * feats, :] = x - hi * LO
        tail = got_ref[s, feats:, :].astype(F32)
        position = jnp.broadcast_to(leaf[s : s + 1], (3, cap))
        columns = jnp.concatenate(
            [jnp.where(position == float(q), tail[:3], 0.0) for q in range(cols // 3)], 0
        )
        w_ref[:, s * cap : (s + 1) * cap] = jnp.concatenate([columns] * HI, 0).astype(BF)
    hi_of = [((iota((16, cap), 0) + 16 * i) // cols).astype(F32).astype(BF) for i in range(HI * cols // 16)]
    lo_of = [(iota((16, cap), 0) + 16 * i).astype(F32).astype(BF) for i in range(LO // 16)]
    one = jnp.ones((), BF)
    zero = jnp.zeros((), BF)

    def step(f, carry):
        res = None
        for k in range(sources // 2):
            a = []
            b = []
            for s in (2 * k, 2 * k + 1):
                hi = hi_ref[pl.ds(s * feats + f, 16, stride=0), :].astype(BF)
                lo = lo_ref[pl.ds(s * feats + f, 16, stride=0), :].astype(BF)
                w = w_ref[:, s * cap : (s + 1) * cap]
                a.append(
                    jnp.concatenate(
                        [jnp.where(hi == of, w[i * 16 : (i + 1) * 16], zero) for i, of in enumerate(hi_of)], 0
                    )
                )
                b.append(jnp.concatenate([jnp.where(lo == of, one, zero) for of in lo_of], 0))
            part = lax.dot_general(
                jnp.concatenate(a, 1), jnp.concatenate(b, 1), NT, preferred_element_type=F32
            )
            res = part if res is None else res + part
        for half in range(2):
            parts = [res[h * cols : (h + 1) * cols] for h in (2 * half, 2 * half + 1)]
            halves[half][pl.ds(f, cols, stride=feats), :] = jnp.concatenate(parts, 1)
        return carry

    lax.fori_loop(0, feats, step, 0, unroll=4)
    size = 3 * feats
    leaf_ref[:, : BINS // 2] = half0_ref[...]
    leaf_ref[:, BINS // 2 :] = half1_ref[...]
    for c in range(cols // 6):
        child_ref[c * size : (c + 1) * size, :] = (
            leaf_ref[2 * c * size : (2 * c + 1) * size, :]
            + leaf_ref[(2 * c + 1) * size : (2 * c + 2) * size, :]
        )
    node_ref[...] = child_ref[:size, :] + child_ref[size:, :]


def specs(space, n):
    return [pl.BlockSpec(memory_space=space)] * n


def on_device(
    binned,
    node_index,
    treatment,
    outcome,
    unit_weight,
    root_feature,
    root_cutoff,
    child_feature,
    child_cutoff,
):
    rows, feats = binned.shape
    nodes = root_feature.shape[0]
    owners = lax.axis_size("rows")
    feat_devices = lax.axis_size("feat")
    cap = 2 * rows // nodes
    depth = feats + 8
    params = pltpu.CompilerParams(vmem_limit_bytes=48 << 20)
    here = lambda name: lax.axis_index(name).astype(jnp.int32)[None]
    rowwise = [binned.T, node_index.T, unit_weight[None], treatment[None], outcome[None]]
    buf, splits = pl.pallas_call(
        place_kernel,
        out_shape=[
            jax.ShapeDtypeStruct((nodes, depth, cap), BF),
            jax.ShapeDtypeStruct((8, cap), jnp.int32),
        ],
        in_specs=specs(pltpu.SMEM, 6) + specs(pltpu.HBM, 5),
        out_specs=specs(pltpu.VMEM, 2),
        scratch_shapes=[
            pltpu.VMEM((feats, rows), jnp.int32),
            pltpu.VMEM((1, rows), jnp.int32),
            pltpu.VMEM((1, rows), F32),
            pltpu.VMEM((1, rows), F32),
            pltpu.VMEM((1, rows), F32),
            pltpu.VMEM((nodes // 2 * depth, rows), BF),
            pltpu.SemaphoreType.DMA((5,)),
        ],
        compiler_params=params,
        name="place",
    )(
        here("rows"), here("feat"), root_feature, root_cutoff, child_feature, child_cutoff,
        *[pltpu.with_memory_space_constraint(x, pltpu.HBM) for x in rowwise],
    )
    got = lax.all_to_all(buf, "rows", 0, 0, tiled=True)
    own = pl.pallas_call(
        split_kernel,
        out_shape=jax.ShapeDtypeStruct((3, owners, cap), BF),
        in_specs=specs(pltpu.VMEM, 2),
        out_specs=specs(pltpu.VMEM, 1)[0],
        compiler_params=params,
        name="split",
    )(splits, got)
    others = [
        lax.ppermute(own, "feat", [(i, (i + k) % feat_devices) for i in range(feat_devices)])
        for k in range(1, feat_devices)
    ]
    shape = lambda n: jax.ShapeDtypeStruct((n * 3 * feats, BINS), F32)
    node_moments, child_moments, leaf_moments = pl.pallas_call(
        hist_kernel,
        out_shape=[shape(1), shape(2), shape(4)],
        in_specs=specs(pltpu.VMEM, 5),
        out_specs=specs(pltpu.VMEM, 3),
        scratch_shapes=[
            pltpu.VMEM((owners * feats, cap), F32),
            pltpu.VMEM((owners * feats, cap), F32),
            pltpu.VMEM((HI * 12, owners * cap), BF),
            pltpu.VMEM((12 * feats, BINS // 2), F32),
            pltpu.VMEM((12 * feats, BINS // 2), F32),
        ],
        compiler_params=params,
        name="hist",
    )(got, own, *others)
    return (
        node_moments.reshape(1, 3, feats, BINS),
        child_moments.reshape(2, 3, feats, BINS),
        leaf_moments.reshape(4, 3, feats, BINS),
    )


def solution(mesh):
    in_specs = (
        P("rows", "feat"),
        P("rows", None),
        P("rows"),
        P("rows"),
        P("rows"),
        P(),
        P(),
        P(),
        P(),
    )
    out_specs = (
        P("rows", None, "feat", None),
        P("rows", None, "feat", None),
        P("rows", None, "feat", None),
    )
    return jax.shard_map(
        on_device, mesh=mesh, in_specs=in_specs, out_specs=out_specs, check_vma=False
    )
```

```python
import jax
import jax.numpy as jnp
from jax import lax
from jax.experimental import pallas as pl
from jax.experimental.pallas import tpu as pltpu
from jax.sharding import PartitionSpec as P

BINS = 256
BF = jnp.bfloat16
F32 = jnp.float32
NT = (((1,), (1,)), ((), ()))
NN = (((1,), (0,)), ((), ()))
HI = 4
LO = BINS // HI
UNROLL = 16
FINISH = 32


def iota(shape, axis):
    return lax.broadcasted_iota(jnp.int32, shape, axis)


def place_kernel(
    owner_ref, place_ref, node_hbm, w_hbm, t_hbm, y_hbm, bins_hbm, rf_hbm, cf_hbm, rc_hbm, cc_hbm,
    out_ref, split_ref, node_ref, w_ref, t_ref, y_ref, bins_ref, rf_ref, cf_ref, rc_ref, cc_ref,
    a_ref, sems,
):
    copies = [
        pltpu.make_async_copy(source, target, sems.at[i])
        for i, (source, target) in enumerate(
            (
                (node_hbm, node_ref), (w_hbm, w_ref), (t_hbm, t_ref), (y_hbm, y_ref),
                (bins_hbm, bins_ref), (rf_hbm, rf_ref), (cf_hbm, cf_ref), (rc_hbm, rc_ref),
                (cc_hbm, cc_ref),
            )
        )
    ]
    for copy in copies:
        copy.start()
    feats, rows = bins_ref.shape
    nodes, depth, cap = out_ref.shape
    blocks = rows // 256
    copies[0].wait()
    node = node_ref[...]
    hot = (iota((nodes, rows), 0) == node).astype(F32)
    stacked = jnp.concatenate([hot[:, b * 256 : (b + 1) * 256] for b in range(blocks)], 0)
    before = (iota((256, 256), 0) < iota((256, 256), 1)).astype(F32).astype(BF)
    ones = jnp.ones((256, 256), BF)
    inner = lax.dot_general(stacked.astype(BF), before, NN, preferred_element_type=F32)
    total = lax.dot_general(stacked.astype(BF), ones, NN, preferred_element_type=F32)
    carry = jnp.zeros((nodes, 256), F32)
    ranks = []
    for b in range(blocks):
        part = slice(b * nodes, (b + 1) * nodes)
        ranks.append(jnp.sum(stacked[part] * (inner[part] + carry), 0, keepdims=True))
        carry = carry + total[part]
    rank = jnp.concatenate(ranks, 1)
    code = rank.astype(jnp.int32) + node % 2 * cap
    slot_hot = (iota((2 * cap, rows), 0) == code).astype(F32).astype(BF)
    for copy in copies[1:4]:
        copy.wait()
    w = w_ref[...]
    t = t_ref[...]
    y = y_ref[...]
    carried = jnp.concatenate([w, w * t * t, w * t * y, jnp.zeros((depth - feats - 3, rows), F32)], 0)
    copies[4].wait()
    bins = jnp.concatenate([bins_ref[...].astype(F32), carried], 0).astype(BF)
    pair = jnp.broadcast_to(node // 2, (depth, rows))
    for p in range(nodes // 2):
        a_ref[p * depth : (p + 1) * depth, :] = jnp.where(pair == p, bins, jnp.zeros((), BF))
    moved = lax.dot_general(a_ref[...], slot_hot, NT, preferred_element_type=F32).astype(BF)
    for p in range(nodes // 2):
        piece = moved[p * depth : (p + 1) * depth]
        out_ref[2 * p] = piece[:, :cap]
        out_ref[2 * p + 1] = piece[:, cap:]
    for copy in copies[5:]:
        copy.wait()
    own = owner_ref[0]
    first = place_ref[0] * feats
    table = [
        rf_ref[own] - first, cf_ref[2 * own] - first, cf_ref[2 * own + 1] - first,
        rc_ref[own], cc_ref[2 * own], cc_ref[2 * own + 1],
    ]
    for k, entry in enumerate(table):
        split_ref[k : k + 1, :] = jnp.full((1, cap), entry, jnp.int32)


def split_kernel(split_ref, got_ref, bits_ref):
    sources, depth, cap = got_ref.shape
    feats = depth - 8
    feature = iota((feats, cap), 0)
    masks = [feature == split_ref[k : k + 1, :] for k in range(3)]
    cutoffs = [split_ref[k : k + 1, :].astype(F32) for k in range(3, 6)]
    rows = [[], [], []]
    for s in range(sources):
        x = got_ref[s, :feats, :].astype(F32)
        for k in range(3):
            right = jnp.where(jnp.logical_and(masks[k], x > cutoffs[k]), 1.0, 0.0)
            rows[k].append(jnp.sum(right, 0, keepdims=True))
    for k in range(3):
        bits_ref[k] = jnp.concatenate(rows[k], 0).astype(BF)


def prepare_kernel(got_ref, hi_ref, lo_ref):
    sources, depth, _ = got_ref.shape
    feats = depth - 8
    for s in range(sources):
        x = got_ref[s, :feats, :].astype(F32)
        hi = jnp.floor(x * (1.0 / LO))
        hi_ref[s * feats : (s + 1) * feats, :] = hi
        lo_ref[s * feats : (s + 1) * feats, :] = x - hi * LO


def hist_kernel(
    got_ref, hi_ref, lo_ref, b0_ref, b1_ref, b2_ref, b3_ref, node_hbm, child_hbm, leaf_hbm, w_ref,
    half0_ref, half1_ref, node_ref, child_ref, leaf_ref, sems,
):
    sources, depth, cap = got_ref.shape
    feats = depth - 8
    cols = leaf_ref.shape[0]
    halves = (half0_ref, half1_ref)
    bits = (b0_ref[...].astype(F32) + b1_ref[...].astype(F32)) + (
        b2_ref[...].astype(F32) + b3_ref[...].astype(F32)
    )
    leaf = 2.0 * bits[0] + jnp.where(bits[0] > 0.5, bits[2], bits[1])
    for s in range(sources):
        tail = got_ref[s, feats:, :].astype(F32)
        position = jnp.broadcast_to(leaf[s : s + 1], (3, cap))
        columns = jnp.concatenate(
            [jnp.where(position == float(q), tail[:3], 0.0) for q in range(cols // 3)], 0
        )
        w_ref[:, s * cap : (s + 1) * cap] = jnp.concatenate([columns] * HI, 0).astype(BF)
    hi_of = [((iota((16, cap), 0) + 16 * i) // cols).astype(F32).astype(BF) for i in range(HI * cols // 16)]
    lo_of = [(iota((16, cap), 0) + 16 * i).astype(F32).astype(BF) for i in range(LO // 16)]
    one = jnp.ones((), BF)
    zero = jnp.zeros((), BF)

    def step(f, carry):
        res = None
        for k in range(sources // 2):
            a = []
            b = []
            for s in (2 * k, 2 * k + 1):
                hi = hi_ref[pl.ds(s * feats + f, 16, stride=0), :].astype(BF)
                lo = lo_ref[pl.ds(s * feats + f, 16, stride=0), :].astype(BF)
                w = w_ref[:, s * cap : (s + 1) * cap]
                a.append(
                    jnp.concatenate(
                        [jnp.where(hi == of, w[i * 16 : (i + 1) * 16], zero) for i, of in enumerate(hi_of)], 0
                    )
                )
                b.append(jnp.concatenate([jnp.where(lo == of, one, zero) for of in lo_of], 0))
            part = lax.dot_general(
                jnp.concatenate(a, 1), jnp.concatenate(b, 1), NT, preferred_element_type=F32
            )
            res = part if res is None else res + part
        for half in range(2):
            parts = [res[h * cols : (h + 1) * cols] for h in (2 * half, 2 * half + 1)]
            halves[half][pl.ds(f, cols, stride=feats), :] = jnp.concatenate(parts, 1)
        return carry

    def outputs(first):
        at = pl.ds(first, FINISH)
        return [
            pltpu.make_async_copy(source.at[:, at, :], target.at[:, at, :], sems.at[first // FINISH, i])
            for i, (source, target) in enumerate(
                ((leaf_ref, leaf_hbm), (child_ref, child_hbm), (node_ref, node_hbm))
            )
        ]

    def group(g, carry):
        first = pl.multiple_of(g * FINISH, FINISH)
        lax.fori_loop(0, FINISH, lambda i, c: step(first + i, c), 0, unroll=UNROLL)
        at = pl.ds(first, FINISH)
        for half in range(2):
            lanes = slice(half * (BINS // 2), (half + 1) * (BINS // 2))
            value = [halves[half][pl.ds(c * feats + first, FINISH), :] for c in range(cols)]
            for c in range(cols):
                leaf_ref[c, at, lanes] = value[c]
            pairs = [value[c] + value[c + 3] for c in (0, 1, 2, 6, 7, 8)]
            for c in range(6):
                child_ref[c, at, lanes] = pairs[c]
            for c in range(3):
                node_ref[c, at, lanes] = pairs[c] + pairs[c + 3]
        for copy in outputs(first):
            copy.start()
        return carry

    lax.fori_loop(0, feats // FINISH, group, 0)
    for g in range(feats // FINISH):
        for copy in outputs(g * FINISH):
            copy.wait()


def specs(space, n):
    return [pl.BlockSpec(memory_space=space)] * n


def on_device(
    binned,
    node_index,
    treatment,
    outcome,
    unit_weight,
    root_feature,
    root_cutoff,
    child_feature,
    child_cutoff,
):
    rows, feats = binned.shape
    nodes = root_feature.shape[0]
    owners = lax.axis_size("rows")
    feat_devices = lax.axis_size("feat")
    cap = 2 * rows // nodes
    depth = feats + 8
    params = pltpu.CompilerParams(vmem_limit_bytes=24 << 20)
    here = lambda name: lax.axis_index(name).astype(jnp.int32)[None]
    sources = [
        node_index.T, unit_weight[None], treatment[None], outcome[None], binned.T,
        root_feature, child_feature, root_cutoff, child_cutoff,
    ]
    buf, splits = pl.pallas_call(
        place_kernel,
        out_shape=[
            jax.ShapeDtypeStruct((nodes, depth, cap), BF),
            jax.ShapeDtypeStruct((8, cap), jnp.int32),
        ],
        in_specs=specs(pltpu.SMEM, 2) + specs(pltpu.HBM, 9),
        out_specs=specs(pltpu.VMEM, 2),
        scratch_shapes=[
            pltpu.VMEM((1, rows), jnp.int32),
            pltpu.VMEM((1, rows), F32),
            pltpu.VMEM((1, rows), F32),
            pltpu.VMEM((1, rows), F32),
            pltpu.VMEM((feats, rows), jnp.int32),
            pltpu.SMEM((nodes,), jnp.int32),
            pltpu.SMEM((2 * nodes,), jnp.int32),
            pltpu.SMEM((nodes,), jnp.int32),
            pltpu.SMEM((2 * nodes,), jnp.int32),
            pltpu.VMEM((nodes // 2 * depth, rows), BF),
            pltpu.SemaphoreType.DMA((9,)),
        ],
        compiler_params=params,
        name="place",
    )(
        here("rows"), here("feat"),
        *[pltpu.with_memory_space_constraint(x, pltpu.HBM) for x in sources],
    )
    got = lax.all_to_all(buf, "rows", 0, 0, tiled=True)
    own = pl.pallas_call(
        split_kernel,
        out_shape=jax.ShapeDtypeStruct((3, owners, cap), BF),
        in_specs=specs(pltpu.VMEM, 2),
        out_specs=specs(pltpu.VMEM, 1)[0],
        compiler_params=params,
        name="split",
    )(splits, got)
    others = [
        lax.ppermute(own, "feat", [(i, (i + k) % feat_devices) for i in range(feat_devices)])
        for k in range(1, feat_devices)
    ]
    digit = jax.ShapeDtypeStruct((owners * feats, cap), F32)
    hi, lo = pl.pallas_call(
        prepare_kernel,
        out_shape=[digit, digit],
        in_specs=specs(pltpu.VMEM, 1),
        out_specs=specs(pltpu.VMEM, 2),
        compiler_params=params,
        name="prepare",
    )(got)
    node_moments, child_moments, leaf_moments = pl.pallas_call(
        hist_kernel,
        out_shape=[jax.ShapeDtypeStruct((n * 3, feats, BINS), F32) for n in (1, 2, 4)],
        in_specs=specs(pltpu.VMEM, 7),
        out_specs=specs(pltpu.HBM, 3),
        scratch_shapes=[
            pltpu.VMEM((HI * 12, owners * cap), BF),
            pltpu.VMEM((12 * feats, BINS // 2), F32),
            pltpu.VMEM((12 * feats, BINS // 2), F32),
            pltpu.VMEM((3, feats, BINS), F32),
            pltpu.VMEM((6, feats, BINS), F32),
            pltpu.VMEM((12, feats, BINS), F32),
            pltpu.SemaphoreType.DMA((feats // FINISH, 3)),
        ],
        compiler_params=params,
        name="hist",
    )(got, hi, lo, own, *others)
    return (
        node_moments.reshape(1, 3, feats, BINS),
        child_moments.reshape(2, 3, feats, BINS),
        leaf_moments.reshape(4, 3, feats, BINS),
    )


def solution(mesh):
    in_specs = (
        P("rows", "feat"),
        P("rows", None),
        P("rows"),
        P("rows"),
        P("rows"),
        P(),
        P(),
        P(),
        P(),
    )
    out_specs = (
        P("rows", None, "feat", None),
        P("rows", None, "feat", None),
        P("rows", None, "feat", None),
    )
    return jax.shard_map(
        on_device, mesh=mesh, in_specs=in_specs, out_specs=out_specs, check_vma=False
    )
```

```python
import jax
import jax.numpy as jnp
from jax import lax
from jax.experimental import pallas as pl
from jax.experimental.pallas import tpu as pltpu
from jax.sharding import PartitionSpec as P

BINS = 256
BF = jnp.bfloat16
F32 = jnp.float32
NT = (((1,), (1,)), ((), ()))
NN = (((1,), (0,)), ((), ()))
HI = 4
LO = BINS // HI
UNROLL = 16
FINISH = 32


def iota(shape, axis):
    return lax.broadcasted_iota(jnp.int32, shape, axis)


def start_all(pairs, sems):
    copies = [pltpu.make_async_copy(pair[0], pair[1], sems.at[i]) for i, pair in enumerate(pairs)]
    for copy in copies:
        copy.start()
    return copies


def decide_kernel(
    place_ref, node_hbm, bins_hbm, rf_hbm, rc_hbm, cf_hbm, cc_hbm, bits_ref, out_ref, node_ref,
    bins_ref, rf_ref, rc_ref, cf_ref, cc_ref, sems,
):
    copies = start_all(
        (
            (node_hbm, node_ref), (rf_hbm, rf_ref), (rc_hbm, rc_ref), (cf_hbm, cf_ref),
            (cc_hbm, cc_ref), (bins_hbm, bins_ref),
        ),
        sems,
    )
    feats, rows = bins_ref.shape
    nodes = rf_ref.shape[1]
    first = place_ref[0] * feats
    for copy in copies[:5]:
        copy.wait()
    node = node_ref[...]

    def look_up(feature_row, cutoff_row, index, count):
        here = (feature_row - first == iota((feats, count), 0)).astype(F32)
        table = jnp.concatenate([here, jnp.broadcast_to(cutoff_row.astype(F32), (8, count))], 0)
        hot = (iota((count, rows), 0) == index).astype(F32).astype(BF)
        return lax.dot_general(table.astype(BF), hot, NN, preferred_element_type=F32)

    got = [
        look_up(rf_ref[...], rc_ref[...], node, nodes),
        look_up(cf_ref[...], cc_ref[...], 2 * node, 2 * nodes),
        look_up(cf_ref[...], cc_ref[...], 2 * node + 1, 2 * nodes),
    ]
    copies[5].wait()
    bins = bins_ref[...].astype(F32)
    out_ref[...] = bins.astype(BF)
    bits = [
        jnp.sum(jnp.where(bins > g[feats : feats + 1], g[:feats], 0.0), 0, keepdims=True) for g in got
    ]
    bits_ref[...] = jnp.concatenate(bits + [jnp.zeros((5, rows), F32)], 0).astype(BF)


def place_kernel(
    bins_ref, node_hbm, w_hbm, t_hbm, y_hbm, out_ref, value_ref, node_ref, w_ref, t_ref, y_ref, a_ref,
    sems,
):
    copies = start_all(((node_hbm, node_ref), (w_hbm, w_ref), (t_hbm, t_ref), (y_hbm, y_ref)), sems)
    feats, rows = bins_ref.shape
    nodes, depth, cap = out_ref.shape
    blocks = rows // 256
    copies[0].wait()
    node = node_ref[...]
    hot = (iota((nodes, rows), 0) == node).astype(F32)
    stacked = jnp.concatenate([hot[:, b * 256 : (b + 1) * 256] for b in range(blocks)], 0)
    before = (iota((256, 256), 0) < iota((256, 256), 1)).astype(F32).astype(BF)
    ones = jnp.ones((256, 256), BF)
    inner = lax.dot_general(stacked.astype(BF), before, NN, preferred_element_type=F32)
    total = lax.dot_general(stacked.astype(BF), ones, NN, preferred_element_type=F32)
    carry = jnp.zeros((nodes, 256), F32)
    ranks = []
    for b in range(blocks):
        part = slice(b * nodes, (b + 1) * nodes)
        ranks.append(jnp.sum(stacked[part] * (inner[part] + carry), 0, keepdims=True))
        carry = carry + total[part]
    rank = jnp.concatenate(ranks, 1)
    code = rank.astype(jnp.int32) + node % 2 * cap
    slot_hot = (iota((2 * cap, rows), 0) == code).astype(F32).astype(BF)
    bins = bins_ref[...]
    pair = jnp.broadcast_to(node // 2, (feats, rows))
    for p in range(nodes // 2):
        a_ref[p * feats : (p + 1) * feats, :] = jnp.where(pair == p, bins, jnp.zeros((), BF))
    moved = lax.dot_general(a_ref[...], slot_hot, NT, preferred_element_type=F32).astype(BF)
    for p in range(nodes // 2):
        piece = moved[p * feats : (p + 1) * feats]
        out_ref[2 * p, :feats, :] = piece[:, :cap]
        out_ref[2 * p + 1, :feats, :] = piece[:, cap:]
    for copy in copies[1:]:
        copy.wait()
    w = w_ref[...]
    t = t_ref[...]
    y = y_ref[...]
    value_ref[...] = jnp.concatenate(
        [w, w * t * t, w * t * y, code.astype(F32), (node // 2).astype(F32), jnp.zeros((3, rows), F32)], 0
    )


def value_kernel(bits_ref, other_ref, value_ref, buf_ref, out_ref, part_ref, sem):
    nodes, _, cap = part_ref.shape
    rows = value_ref.shape[1]
    bits = bits_ref[...].astype(F32) + other_ref[...].astype(F32)
    carried = jnp.concatenate([value_ref[:3, :], bits[:5]], 0)
    code = value_ref[3:4, :].astype(jnp.int32)
    slot_hot = (iota((2 * cap, rows), 0) == code).astype(F32).astype(BF)
    pair = jnp.broadcast_to(value_ref[4:5, :], (8, rows))
    spread = jnp.concatenate(
        [jnp.where(pair == float(p), carried, 0.0) for p in range(nodes // 2)], 0
    ).astype(BF)
    moved = lax.dot_general(spread, slot_hot, NT, preferred_element_type=F32).astype(BF)
    for p in range(nodes // 2):
        piece = moved[p * 8 : (p + 1) * 8]
        part_ref[2 * p] = piece[:, :cap]
        part_ref[2 * p + 1] = piece[:, cap:]
    copy = pltpu.make_async_copy(part_ref, out_ref.at[:, pl.ds(out_ref.shape[1] - 8, 8), :], sem)
    copy.start()
    copy.wait()


def tail_kernel(got_ref, bits_ref):
    sources, depth, _ = got_ref.shape
    tails = [got_ref[s, depth - 8 :, :].astype(F32) for s in range(sources)]
    for k in range(3):
        bits_ref[k] = jnp.concatenate([tail[3 + k : 4 + k] for tail in tails], 0).astype(BF)


def prepare_kernel(got_ref, hi_ref, lo_ref):
    sources, depth, _ = got_ref.shape
    feats = depth - 8
    for s in range(sources):
        x = got_ref[s, :feats, :].astype(F32)
        hi = jnp.floor(x * (1.0 / LO))
        hi_ref[s * feats : (s + 1) * feats, :] = hi
        lo_ref[s * feats : (s + 1) * feats, :] = x - hi * LO


def hist_kernel(
    got_ref, hi_ref, lo_ref, bits_ref, other_ref, node_hbm, child_hbm, leaf_hbm, w_ref, half0_ref,
    half1_ref, node_ref, child_ref, leaf_ref, sems,
):
    sources, depth, cap = got_ref.shape
    feats = depth - 8
    cols = leaf_ref.shape[0]
    halves = (half0_ref, half1_ref)
    bits = bits_ref[...].astype(F32) + other_ref[...].astype(F32)
    leaf = 2.0 * bits[0] + jnp.where(bits[0] > 0.5, bits[2], bits[1])
    for s in range(sources):
        tail = got_ref[s, feats:, :].astype(F32)
        position = jnp.broadcast_to(leaf[s : s + 1], (3, cap))
        columns = jnp.concatenate(
            [jnp.where(position == float(q), tail[:3], 0.0) for q in range(cols // 3)], 0
        )
        w_ref[:, s * cap : (s + 1) * cap] = jnp.concatenate([columns] * HI, 0).astype(BF)
    hi_of = [((iota((16, cap), 0) + 16 * i) // cols).astype(F32).astype(BF) for i in range(HI * cols // 16)]
    lo_of = [(iota((16, cap), 0) + 16 * i).astype(F32).astype(BF) for i in range(LO // 16)]
    one = jnp.ones((), BF)
    zero = jnp.zeros((), BF)

    def step(f, carry):
        res = None
        for k in range(sources // 2):
            a = []
            b = []
            for s in (2 * k, 2 * k + 1):
                hi = hi_ref[pl.ds(s * feats + f, 16, stride=0), :].astype(BF)
                lo = lo_ref[pl.ds(s * feats + f, 16, stride=0), :].astype(BF)
                w = w_ref[:, s * cap : (s + 1) * cap]
                a.append(
                    jnp.concatenate(
                        [jnp.where(hi == of, w[i * 16 : (i + 1) * 16], zero) for i, of in enumerate(hi_of)], 0
                    )
                )
                b.append(jnp.concatenate([jnp.where(lo == of, one, zero) for of in lo_of], 0))
            part = lax.dot_general(
                jnp.concatenate(a, 1), jnp.concatenate(b, 1), NT, preferred_element_type=F32
            )
            res = part if res is None else res + part
        for half in range(2):
            parts = [res[h * cols : (h + 1) * cols] for h in (2 * half, 2 * half + 1)]
            halves[half][pl.ds(f, cols, stride=feats), :] = jnp.concatenate(parts, 1)
        return carry

    def outputs(first):
        at = pl.ds(first, FINISH)
        return [
            pltpu.make_async_copy(source.at[:, at, :], target.at[:, at, :], sems.at[first // FINISH, i])
            for i, (source, target) in enumerate(
                ((leaf_ref, leaf_hbm), (child_ref, child_hbm), (node_ref, node_hbm))
            )
        ]

    def group(g, carry):
        first = pl.multiple_of(g * FINISH, FINISH)
        lax.fori_loop(0, FINISH, lambda i, c: step(first + i, c), 0, unroll=UNROLL)
        at = pl.ds(first, FINISH)
        for half in range(2):
            lanes = slice(half * (BINS // 2), (half + 1) * (BINS // 2))
            value = [halves[half][pl.ds(c * feats + first, FINISH), :] for c in range(cols)]
            for c in range(cols):
                leaf_ref[c, at, lanes] = value[c]
            pairs = [value[c] + value[c + 3] for c in (0, 1, 2, 6, 7, 8)]
            for c in range(6):
                child_ref[c, at, lanes] = pairs[c]
            for c in range(3):
                node_ref[c, at, lanes] = pairs[c] + pairs[c + 3]
        for copy in outputs(first):
            copy.start()
        return carry

    lax.fori_loop(0, feats // FINISH, group, 0)
    for g in range(feats // FINISH):
        for copy in outputs(g * FINISH):
            copy.wait()


def specs(space, n):
    return [pl.BlockSpec(memory_space=space)] * n


def on_device(
    binned,
    node_index,
    treatment,
    outcome,
    unit_weight,
    root_feature,
    root_cutoff,
    child_feature,
    child_cutoff,
):
    rows, feats = binned.shape
    nodes = root_feature.shape[0]
    owners = lax.axis_size("rows")
    feat_devices = lax.axis_size("feat")
    cap = 2 * rows // nodes
    depth = feats + 8
    params = pltpu.CompilerParams(vmem_limit_bytes=24 << 20)
    in_hbm = lambda *xs: [pltpu.with_memory_space_constraint(x, pltpu.HBM) for x in xs]
    row = lambda dtype: pltpu.VMEM((1, rows), dtype)
    swap = lambda x, bit: lax.ppermute(x, "feat", [(i, i ^ bit) for i in range(feat_devices)])
    bins, node = in_hbm(binned.T, node_index.T)
    own, narrow = pl.pallas_call(
        decide_kernel,
        out_shape=[jax.ShapeDtypeStruct((8, rows), BF), jax.ShapeDtypeStruct((feats, rows), BF)],
        in_specs=specs(pltpu.SMEM, 1) + specs(pltpu.HBM, 6),
        out_specs=specs(pltpu.VMEM, 2),
        scratch_shapes=[
            row(jnp.int32),
            pltpu.VMEM((feats, rows), jnp.int32),
            pltpu.VMEM((1, nodes), jnp.int32),
            pltpu.VMEM((1, nodes), jnp.int32),
            pltpu.VMEM((1, 2 * nodes), jnp.int32),
            pltpu.VMEM((1, 2 * nodes), jnp.int32),
            pltpu.SemaphoreType.DMA((6,)),
        ],
        compiler_params=params,
        name="decide",
    )(
        lax.axis_index("feat").astype(jnp.int32)[None], node, bins,
        *in_hbm(root_feature[None], root_cutoff[None], child_feature[None], child_cutoff[None]),
    )
    other = swap(own, 1)
    buf, value = pl.pallas_call(
        place_kernel,
        out_shape=[
            jax.ShapeDtypeStruct((nodes, depth, cap), BF),
            jax.ShapeDtypeStruct((8, rows), F32),
        ],
        in_specs=specs(pltpu.VMEM, 1) + specs(pltpu.HBM, 4),
        out_specs=specs(pltpu.VMEM, 2),
        scratch_shapes=[
            row(jnp.int32), row(F32), row(F32), row(F32),
            pltpu.VMEM((nodes // 2 * feats, rows), BF),
            pltpu.SemaphoreType.DMA((4,)),
        ],
        compiler_params=params,
        name="place",
    )(narrow, node, *in_hbm(unit_weight[None], treatment[None], outcome[None]))
    buf = pl.pallas_call(
        value_kernel,
        out_shape=jax.ShapeDtypeStruct((nodes, depth, cap), BF),
        in_specs=specs(pltpu.VMEM, 3) + specs(pl.ANY, 1),
        out_specs=specs(pl.ANY, 1)[0],
        scratch_shapes=[pltpu.VMEM((nodes, 8, cap), BF), pltpu.SemaphoreType.DMA],
        input_output_aliases={3: 0},
        compiler_params=params,
        name="value",
    )(own, other, value, buf)
    got = lax.all_to_all(buf, "rows", 0, 0, tiled=True)
    half = pl.pallas_call(
        tail_kernel,
        out_shape=jax.ShapeDtypeStruct((3, owners, cap), BF),
        in_specs=specs(pltpu.VMEM, 1),
        out_specs=specs(pltpu.VMEM, 1)[0],
        compiler_params=params,
        name="tail",
    )(got)
    rest = swap(half, 2)
    digit = jax.ShapeDtypeStruct((owners * feats, cap), F32)
    hi, lo = pl.pallas_call(
        prepare_kernel,
        out_shape=[digit, digit],
        in_specs=specs(pltpu.VMEM, 1),
        out_specs=specs(pltpu.VMEM, 2),
        compiler_params=params,
        name="prepare",
    )(got)
    node_moments, child_moments, leaf_moments = pl.pallas_call(
        hist_kernel,
        out_shape=[jax.ShapeDtypeStruct((n * 3, feats, BINS), F32) for n in (1, 2, 4)],
        in_specs=specs(pltpu.VMEM, 5),
        out_specs=specs(pltpu.HBM, 3),
        scratch_shapes=[
            pltpu.VMEM((HI * 12, owners * cap), BF),
            pltpu.VMEM((12 * feats, BINS // 2), F32),
            pltpu.VMEM((12 * feats, BINS // 2), F32),
            pltpu.VMEM((3, feats, BINS), F32),
            pltpu.VMEM((6, feats, BINS), F32),
            pltpu.VMEM((12, feats, BINS), F32),
            pltpu.SemaphoreType.DMA((feats // FINISH, 3)),
        ],
        compiler_params=params,
        name="hist",
    )(got, hi, lo, half, rest)
    return (
        node_moments.reshape(1, 3, feats, BINS),
        child_moments.reshape(2, 3, feats, BINS),
        leaf_moments.reshape(4, 3, feats, BINS),
    )


def solution(mesh):
    in_specs = (
        P("rows", "feat"),
        P("rows", None),
        P("rows"),
        P("rows"),
        P("rows"),
        P(),
        P(),
        P(),
        P(),
    )
    out_specs = (
        P("rows", None, "feat", None),
        P("rows", None, "feat", None),
        P("rows", None, "feat", None),
    )
    return jax.shard_map(
        on_device, mesh=mesh, in_specs=in_specs, out_specs=out_specs, check_vma=False
    )
```

```python
import jax
import jax.numpy as jnp
from jax import lax
from jax.experimental import pallas as pl
from jax.experimental.pallas import tpu as pltpu
from jax.sharding import PartitionSpec as P

BINS = 256
BF = jnp.bfloat16
F32 = jnp.float32
NT = (((1,), (1,)), ((), ()))
NN = (((1,), (0,)), ((), ()))
HI = 4
LO = BINS // HI
UNROLL = 32
FINISH = 32


def iota(shape, axis):
    return lax.broadcasted_iota(jnp.int32, shape, axis)


def start_all(pairs, sems):
    copies = [pltpu.make_async_copy(pair[0], pair[1], sems.at[i]) for i, pair in enumerate(pairs)]
    for copy in copies:
        copy.start()
    return copies


def decide_kernel(
    place_ref, node_hbm, bins_hbm, rf_hbm, rc_hbm, cf_hbm, cc_hbm, bits_ref, out_ref, node_ref,
    bins_ref, rf_ref, rc_ref, cf_ref, cc_ref, sems,
):
    copies = start_all(
        (
            (node_hbm, node_ref), (rf_hbm, rf_ref), (rc_hbm, rc_ref), (cf_hbm, cf_ref),
            (cc_hbm, cc_ref), (bins_hbm, bins_ref),
        ),
        sems,
    )
    feats, rows = bins_ref.shape
    nodes = rf_ref.shape[1]
    first = place_ref[0] * feats
    for copy in copies[:5]:
        copy.wait()
    node = node_ref[...]

    def look_up(feature_row, cutoff_row, index, count):
        here = (feature_row - first == iota((feats, count), 0)).astype(F32)
        table = jnp.concatenate([here, jnp.broadcast_to(cutoff_row.astype(F32), (8, count))], 0)
        hot = (iota((count, rows), 0) == index).astype(F32).astype(BF)
        return lax.dot_general(table.astype(BF), hot, NN, preferred_element_type=F32)

    got = [
        look_up(rf_ref[...], rc_ref[...], node, nodes),
        look_up(cf_ref[...], cc_ref[...], 2 * node, 2 * nodes),
        look_up(cf_ref[...], cc_ref[...], 2 * node + 1, 2 * nodes),
    ]
    copies[5].wait()
    bins = bins_ref[...].astype(F32)
    out_ref[...] = bins.astype(BF)
    bits = [
        jnp.sum(jnp.where(bins > g[feats : feats + 1], g[:feats], 0.0), 0, keepdims=True) for g in got
    ]
    bits_ref[...] = jnp.concatenate(bits + [jnp.zeros((5, rows), F32)], 0).astype(BF)


def place_kernel(
    bins_ref, node_hbm, w_hbm, t_hbm, y_hbm, out_ref, value_ref, node_ref, w_ref, t_ref, y_ref, a_ref,
    sems,
):
    copies = start_all(((node_hbm, node_ref), (w_hbm, w_ref), (t_hbm, t_ref), (y_hbm, y_ref)), sems)
    feats, rows = bins_ref.shape
    nodes, depth, cap = out_ref.shape
    blocks = rows // 256
    copies[0].wait()
    node = node_ref[...]
    hot = (iota((nodes, rows), 0) == node).astype(F32)
    stacked = jnp.concatenate([hot[:, b * 256 : (b + 1) * 256] for b in range(blocks)], 0)
    before = (iota((256, 256), 0) < iota((256, 256), 1)).astype(F32).astype(BF)
    ones = jnp.ones((256, 256), BF)
    inner = lax.dot_general(stacked.astype(BF), before, NN, preferred_element_type=F32)
    total = lax.dot_general(stacked.astype(BF), ones, NN, preferred_element_type=F32)
    carry = jnp.zeros((nodes, 256), F32)
    ranks = []
    for b in range(blocks):
        part = slice(b * nodes, (b + 1) * nodes)
        ranks.append(jnp.sum(stacked[part] * (inner[part] + carry), 0, keepdims=True))
        carry = carry + total[part]
    rank = jnp.concatenate(ranks, 1)
    code = rank.astype(jnp.int32) + node % 2 * cap
    slot_hot = (iota((2 * cap, rows), 0) == code).astype(F32).astype(BF)
    bins = bins_ref[...]
    pair = jnp.broadcast_to(node // 2, (feats, rows))
    for p in range(nodes // 2):
        a_ref[p * feats : (p + 1) * feats, :] = jnp.where(pair == p, bins, jnp.zeros((), BF))
    moved = lax.dot_general(a_ref[...], slot_hot, NT, preferred_element_type=F32).astype(BF)
    for p in range(nodes // 2):
        piece = moved[p * feats : (p + 1) * feats]
        out_ref[2 * p, :feats, :] = piece[:, :cap]
        out_ref[2 * p + 1, :feats, :] = piece[:, cap:]
    for copy in copies[1:]:
        copy.wait()
    w = w_ref[...]
    t = t_ref[...]
    y = y_ref[...]
    value_ref[...] = jnp.concatenate(
        [w, w * t * t, w * t * y, code.astype(F32), (node // 2).astype(F32), jnp.zeros((3, rows), F32)], 0
    )


def value_kernel(bits_ref, other_ref, value_ref, buf_ref, out_ref, part_ref, sem):
    nodes, _, cap = part_ref.shape
    rows = value_ref.shape[1]
    bits = bits_ref[...].astype(F32) + other_ref[...].astype(F32)
    carried = jnp.concatenate([value_ref[:3, :], bits[:5]], 0)
    code = value_ref[3:4, :].astype(jnp.int32)
    slot_hot = (iota((2 * cap, rows), 0) == code).astype(F32).astype(BF)
    pair = jnp.broadcast_to(value_ref[4:5, :], (8, rows))
    spread = jnp.concatenate(
        [jnp.where(pair == float(p), carried, 0.0) for p in range(nodes // 2)], 0
    ).astype(BF)
    moved = lax.dot_general(spread, slot_hot, NT, preferred_element_type=F32).astype(BF)
    for p in range(nodes // 2):
        piece = moved[p * 8 : (p + 1) * 8]
        part_ref[2 * p] = piece[:, :cap]
        part_ref[2 * p + 1] = piece[:, cap:]
    copy = pltpu.make_async_copy(part_ref, out_ref.at[:, pl.ds(out_ref.shape[1] - 8, 8), :], sem)
    copy.start()
    copy.wait()


def tail_kernel(got_ref, bits_ref):
    sources, depth, _ = got_ref.shape
    tails = [got_ref[s, depth - 8 :, :].astype(F32) for s in range(sources)]
    for k in range(3):
        bits_ref[k] = jnp.concatenate([tail[3 + k : 4 + k] for tail in tails], 0).astype(BF)


def prepare_kernel(got_ref, hi_ref, lo_ref):
    sources, depth, _ = got_ref.shape
    feats = depth - 8
    for s in range(sources):
        x = got_ref[s, :feats, :].astype(F32)
        hi = jnp.floor(x * (1.0 / LO))
        hi_ref[s * feats : (s + 1) * feats, :] = hi
        lo_ref[s * feats : (s + 1) * feats, :] = x - hi * LO


def hist_kernel(
    got_ref, hi_ref, lo_ref, bits_ref, other_ref, node_hbm, child_hbm, leaf_hbm, w_ref, half0_ref,
    half1_ref, node_ref, child_ref, leaf_ref, sems,
):
    sources, depth, cap = got_ref.shape
    feats = depth - 8
    cols = leaf_ref.shape[0]
    halves = (half0_ref, half1_ref)
    bits = bits_ref[...].astype(F32) + other_ref[...].astype(F32)
    leaf = 2.0 * bits[0] + jnp.where(bits[0] > 0.5, bits[2], bits[1])
    for s in range(sources):
        tail = got_ref[s, feats:, :].astype(F32)
        position = jnp.broadcast_to(leaf[s : s + 1], (3, cap))
        columns = jnp.concatenate(
            [jnp.where(position == float(q), tail[:3], 0.0) for q in range(cols // 3)], 0
        )
        w_ref[:, s * cap : (s + 1) * cap] = jnp.concatenate([columns] * HI, 0).astype(BF)
    hi_of = [((iota((16, cap), 0) + 16 * i) // cols).astype(F32).astype(BF) for i in range(HI * cols // 16)]
    lo_of = [(iota((16, cap), 0) + 16 * i).astype(F32).astype(BF) for i in range(LO // 16)]
    one = jnp.ones((), BF)
    zero = jnp.zeros((), BF)

    def step(f, carry):
        res = None
        for k in range(sources // 2):
            a = []
            b = []
            for s in (2 * k, 2 * k + 1):
                hi = hi_ref[pl.ds(s * feats + f, 16, stride=0), :].astype(BF)
                lo = lo_ref[pl.ds(s * feats + f, 16, stride=0), :].astype(BF)
                w = w_ref[:, s * cap : (s + 1) * cap]
                a.append(
                    jnp.concatenate(
                        [jnp.where(hi == of, w[i * 16 : (i + 1) * 16], zero) for i, of in enumerate(hi_of)], 0
                    )
                )
                b.append(jnp.concatenate([jnp.where(lo == of, one, zero) for of in lo_of], 0))
            part = lax.dot_general(
                jnp.concatenate(a, 1), jnp.concatenate(b, 1), NT, preferred_element_type=F32
            )
            res = part if res is None else res + part
        for half in range(2):
            parts = [res[h * cols : (h + 1) * cols] for h in (2 * half, 2 * half + 1)]
            halves[half][pl.ds(f, cols, stride=feats), :] = jnp.concatenate(parts, 1)
        return carry

    def outputs(first):
        at = pl.ds(first, FINISH)
        return [
            pltpu.make_async_copy(source.at[:, at, :], target.at[:, at, :], sems.at[first // FINISH, i])
            for i, (source, target) in enumerate(
                ((leaf_ref, leaf_hbm), (child_ref, child_hbm), (node_ref, node_hbm))
            )
        ]

    def group(g, carry):
        first = pl.multiple_of(g * FINISH, FINISH)
        lax.fori_loop(0, FINISH, lambda i, c: step(first + i, c), 0, unroll=UNROLL)
        at = pl.ds(first, FINISH)
        for half in range(2):
            lanes = slice(half * (BINS // 2), (half + 1) * (BINS // 2))
            value = [halves[half][pl.ds(c * feats + first, FINISH), :] for c in range(cols)]
            for c in range(cols):
                leaf_ref[c, at, lanes] = value[c]
            pairs = [value[c] + value[c + 3] for c in (0, 1, 2, 6, 7, 8)]
            for c in range(6):
                child_ref[c, at, lanes] = pairs[c]
            for c in range(3):
                node_ref[c, at, lanes] = pairs[c] + pairs[c + 3]
        for copy in outputs(first):
            copy.start()
        return carry

    lax.fori_loop(0, feats // FINISH, group, 0)
    for g in range(feats // FINISH):
        for copy in outputs(g * FINISH):
            copy.wait()


def specs(space, n):
    return [pl.BlockSpec(memory_space=space)] * n


def on_device(
    binned,
    node_index,
    treatment,
    outcome,
    unit_weight,
    root_feature,
    root_cutoff,
    child_feature,
    child_cutoff,
):
    rows, feats = binned.shape
    nodes = root_feature.shape[0]
    owners = lax.axis_size("rows")
    feat_devices = lax.axis_size("feat")
    cap = 2 * rows // nodes
    depth = feats + 8
    params = pltpu.CompilerParams(vmem_limit_bytes=24 << 20)
    in_hbm = lambda *xs: [pltpu.with_memory_space_constraint(x, pltpu.HBM) for x in xs]
    row = lambda dtype: pltpu.VMEM((1, rows), dtype)
    swap = lambda x, bit: lax.ppermute(x, "feat", [(i, i ^ bit) for i in range(feat_devices)])
    bins, node = in_hbm(binned.T, node_index.T)
    own, narrow = pl.pallas_call(
        decide_kernel,
        out_shape=[jax.ShapeDtypeStruct((8, rows), BF), jax.ShapeDtypeStruct((feats, rows), BF)],
        in_specs=specs(pltpu.SMEM, 1) + specs(pltpu.HBM, 6),
        out_specs=specs(pltpu.VMEM, 2),
        scratch_shapes=[
            row(jnp.int32),
            pltpu.VMEM((feats, rows), jnp.int32),
            pltpu.VMEM((1, nodes), jnp.int32),
            pltpu.VMEM((1, nodes), jnp.int32),
            pltpu.VMEM((1, 2 * nodes), jnp.int32),
            pltpu.VMEM((1, 2 * nodes), jnp.int32),
            pltpu.SemaphoreType.DMA((6,)),
        ],
        compiler_params=params,
        name="decide",
    )(
        lax.axis_index("feat").astype(jnp.int32)[None], node, bins,
        *in_hbm(root_feature[None], root_cutoff[None], child_feature[None], child_cutoff[None]),
    )
    other = swap(own, 1)
    buf, value = pl.pallas_call(
        place_kernel,
        out_shape=[
            jax.ShapeDtypeStruct((nodes, depth, cap), BF),
            jax.ShapeDtypeStruct((8, rows), F32),
        ],
        in_specs=specs(pltpu.VMEM, 1) + specs(pltpu.HBM, 4),
        out_specs=specs(pltpu.VMEM, 2),
        scratch_shapes=[
            row(jnp.int32), row(F32), row(F32), row(F32),
            pltpu.VMEM((nodes // 2 * feats, rows), BF),
            pltpu.SemaphoreType.DMA((4,)),
        ],
        compiler_params=params,
        name="place",
    )(narrow, node, *in_hbm(unit_weight[None], treatment[None], outcome[None]))
    buf = pl.pallas_call(
        value_kernel,
        out_shape=jax.ShapeDtypeStruct((nodes, depth, cap), BF),
        in_specs=specs(pltpu.VMEM, 3) + specs(pl.ANY, 1),
        out_specs=specs(pl.ANY, 1)[0],
        scratch_shapes=[pltpu.VMEM((nodes, 8, cap), BF), pltpu.SemaphoreType.DMA],
        input_output_aliases={3: 0},
        compiler_params=params,
        name="value",
    )(own, other, value, buf)
    got = lax.all_to_all(buf, "rows", 0, 0, tiled=True)
    half = pl.pallas_call(
        tail_kernel,
        out_shape=jax.ShapeDtypeStruct((3, owners, cap), BF),
        in_specs=specs(pltpu.VMEM, 1),
        out_specs=specs(pltpu.VMEM, 1)[0],
        compiler_params=params,
        name="tail",
    )(got)
    rest = swap(half, 3)
    digit = jax.ShapeDtypeStruct((owners * feats, cap), F32)
    hi, lo = pl.pallas_call(
        prepare_kernel,
        out_shape=[digit, digit],
        in_specs=specs(pltpu.VMEM, 1),
        out_specs=specs(pltpu.VMEM, 2),
        compiler_params=params,
        name="prepare",
    )(got)
    node_moments, child_moments, leaf_moments = pl.pallas_call(
        hist_kernel,
        out_shape=[jax.ShapeDtypeStruct((n * 3, feats, BINS), F32) for n in (1, 2, 4)],
        in_specs=specs(pltpu.VMEM, 5),
        out_specs=specs(pltpu.HBM, 3),
        scratch_shapes=[
            pltpu.VMEM((HI * 12, owners * cap), BF),
            pltpu.VMEM((12 * feats, BINS // 2), F32),
            pltpu.VMEM((12 * feats, BINS // 2), F32),
            pltpu.VMEM((3, feats, BINS), F32),
            pltpu.VMEM((6, feats, BINS), F32),
            pltpu.VMEM((12, feats, BINS), F32),
            pltpu.SemaphoreType.DMA((feats // FINISH, 3)),
        ],
        compiler_params=params,
        name="hist",
    )(got, hi, lo, half, rest)
    return (
        node_moments.reshape(1, 3, feats, BINS),
        child_moments.reshape(2, 3, feats, BINS),
        leaf_moments.reshape(4, 3, feats, BINS),
    )


def solution(mesh):
    in_specs = (
        P("rows", "feat"),
        P("rows", None),
        P("rows"),
        P("rows"),
        P("rows"),
        P(),
        P(),
        P(),
        P(),
    )
    out_specs = (
        P("rows", None, "feat", None),
        P("rows", None, "feat", None),
        P("rows", None, "feat", None),
    )
    return jax.shard_map(
        on_device, mesh=mesh, in_specs=in_specs, out_specs=out_specs, check_vma=False
    )
```

```python
import jax
import jax.numpy as jnp
from jax import lax
from jax.experimental import pallas as pl
from jax.experimental.pallas import tpu as pltpu
from jax.sharding import PartitionSpec as P

BINS = 256
BF = jnp.bfloat16
F32 = jnp.float32
NT = (((1,), (1,)), ((), ()))
NN = (((1,), (0,)), ((), ()))
HI = 4
LO = BINS // HI
FINISH = 16


def iota(shape, axis):
    return lax.broadcasted_iota(jnp.int32, shape, axis)


def start_all(pairs, sems):
    copies = [pltpu.make_async_copy(pair[0], pair[1], sems.at[i]) for i, pair in enumerate(pairs)]
    for copy in copies:
        copy.start()
    return copies


def decide_kernel(
    place_ref, node_hbm, bins_hbm, rf_hbm, rc_hbm, cf_hbm, cc_hbm, bits_ref, out_ref, node_ref,
    bins_ref, rf_ref, rc_ref, cf_ref, cc_ref, sems,
):
    copies = start_all(
        (
            (node_hbm, node_ref), (rf_hbm, rf_ref), (rc_hbm, rc_ref), (cf_hbm, cf_ref),
            (cc_hbm, cc_ref), (bins_hbm, bins_ref),
        ),
        sems,
    )
    feats, rows = bins_ref.shape
    nodes = rf_ref.shape[1]
    first = place_ref[0] * feats
    for copy in copies[:5]:
        copy.wait()
    node = node_ref[...]

    def look_up(feature_row, cutoff_row, index, count):
        here = (feature_row - first == iota((feats, count), 0)).astype(F32)
        table = jnp.concatenate([here, jnp.broadcast_to(cutoff_row.astype(F32), (8, count))], 0)
        hot = (iota((count, rows), 0) == index).astype(F32).astype(BF)
        return lax.dot_general(table.astype(BF), hot, NN, preferred_element_type=F32)

    got = [
        look_up(rf_ref[...], rc_ref[...], node, nodes),
        look_up(cf_ref[...], cc_ref[...], 2 * node, 2 * nodes),
        look_up(cf_ref[...], cc_ref[...], 2 * node + 1, 2 * nodes),
    ]
    copies[5].wait()
    bins = bins_ref[...].astype(F32)
    out_ref[...] = bins.astype(BF)
    bits = [
        jnp.sum(jnp.where(bins > g[feats : feats + 1], g[:feats], 0.0), 0, keepdims=True) for g in got
    ]
    bits_ref[...] = jnp.concatenate(bits + [jnp.zeros((5, rows), F32)], 0).astype(BF)


def place_kernel(
    bins_ref, node_hbm, w_hbm, t_hbm, y_hbm, out_ref, value_ref, node_ref, w_ref, t_ref, y_ref, a_ref,
    sems,
):
    copies = start_all(((node_hbm, node_ref), (w_hbm, w_ref), (t_hbm, t_ref), (y_hbm, y_ref)), sems)
    feats, rows = bins_ref.shape
    nodes, depth, cap = out_ref.shape
    blocks = rows // 256
    copies[0].wait()
    node = node_ref[...]
    hot = (iota((nodes, rows), 0) == node).astype(F32)
    stacked = jnp.concatenate([hot[:, b * 256 : (b + 1) * 256] for b in range(blocks)], 0)
    before = (iota((256, 256), 0) < iota((256, 256), 1)).astype(F32).astype(BF)
    ones = jnp.ones((256, 256), BF)
    inner = lax.dot_general(stacked.astype(BF), before, NN, preferred_element_type=F32)
    total = lax.dot_general(stacked.astype(BF), ones, NN, preferred_element_type=F32)
    carry = jnp.zeros((nodes, 256), F32)
    ranks = []
    for b in range(blocks):
        part = slice(b * nodes, (b + 1) * nodes)
        ranks.append(jnp.sum(stacked[part] * (inner[part] + carry), 0, keepdims=True))
        carry = carry + total[part]
    rank = jnp.concatenate(ranks, 1)
    code = rank.astype(jnp.int32) + node % 2 * cap
    slot_hot = (iota((2 * cap, rows), 0) == code).astype(F32).astype(BF)
    bins = bins_ref[...]
    pair = jnp.broadcast_to(node // 2, (feats, rows))
    for p in range(nodes // 2):
        a_ref[p * feats : (p + 1) * feats, :] = jnp.where(pair == p, bins, jnp.zeros((), BF))
    moved = lax.dot_general(a_ref[...], slot_hot, NT, preferred_element_type=F32).astype(BF)
    for p in range(nodes // 2):
        piece = moved[p * feats : (p + 1) * feats]
        out_ref[2 * p, :feats, :] = piece[:, :cap]
        out_ref[2 * p + 1, :feats, :] = piece[:, cap:]
    for copy in copies[1:]:
        copy.wait()
    w = w_ref[...]
    t = t_ref[...]
    y = y_ref[...]
    value_ref[...] = jnp.concatenate(
        [w, w * t * t, w * t * y, code.astype(F32), (node // 2).astype(F32), jnp.zeros((3, rows), F32)], 0
    )


def value_kernel(bits_ref, other_ref, value_ref, buf_ref, out_ref, part_ref, sem):
    nodes, _, cap = part_ref.shape
    rows = value_ref.shape[1]
    bits = bits_ref[...].astype(F32) + other_ref[...].astype(F32)
    carried = jnp.concatenate([value_ref[:3, :], bits[:5]], 0)
    code = value_ref[3:4, :].astype(jnp.int32)
    slot_hot = (iota((2 * cap, rows), 0) == code).astype(F32).astype(BF)
    pair = jnp.broadcast_to(value_ref[4:5, :], (8, rows))
    spread = jnp.concatenate(
        [jnp.where(pair == float(p), carried, 0.0) for p in range(nodes // 2)], 0
    ).astype(BF)
    moved = lax.dot_general(spread, slot_hot, NT, preferred_element_type=F32).astype(BF)
    for p in range(nodes // 2):
        piece = moved[p * 8 : (p + 1) * 8]
        part_ref[2 * p] = piece[:, :cap]
        part_ref[2 * p + 1] = piece[:, cap:]
    copy = pltpu.make_async_copy(part_ref, out_ref.at[:, pl.ds(out_ref.shape[1] - 8, 8), :], sem)
    copy.start()
    copy.wait()


def tail_kernel(got_ref, bits_ref):
    sources, depth, _ = got_ref.shape
    tails = [got_ref[s, depth - 8 :, :].astype(F32) for s in range(sources)]
    for k in range(3):
        bits_ref[k] = jnp.concatenate([tail[3 + k : 4 + k] for tail in tails], 0).astype(BF)


def prepare_kernel(got_ref, hi_ref, lo_ref, moment_ref):
    sources, depth, cap = got_ref.shape
    feats = depth - 8
    which = iota((moment_ref.shape[0], cap), 0) % 3
    for s in range(sources):
        x = got_ref[s, :feats, :].astype(F32)
        hi = jnp.floor(x * (1.0 / LO))
        hi_ref[s * feats : (s + 1) * feats, :] = hi
        lo_ref[s * feats : (s + 1) * feats, :] = x - hi * LO
        tail = got_ref[s, feats:, :].astype(F32)
        moments = jnp.where(which == 0, tail[0:1], jnp.where(which == 1, tail[1:2], tail[2:3]))
        moment_ref[:, s * cap : (s + 1) * cap] = moments.astype(BF)


def hist_kernel(
    hi_ref, lo_ref, moment_ref, bits_ref, other_ref, node_hbm, child_hbm, leaf_hbm, w_ref, half0_ref,
    half1_ref, node_ref, child_ref, leaf_ref, sems,
):
    cols, feats, _ = leaf_ref.shape
    _, sources, cap = bits_ref.shape
    halves = (half0_ref, half1_ref)
    one = jnp.ones((), BF)
    zero = jnp.zeros((), BF)
    bits = bits_ref[...].astype(F32) + other_ref[...].astype(F32)
    leaf = 2.0 * bits[0] + jnp.where(bits[0] > 0.5, bits[2], bits[1])
    leaf_of = (iota((HI * cols, cap), 0) % cols // 3).astype(F32).astype(BF)
    for s in range(sources):
        at = slice(s * cap, (s + 1) * cap)
        position = jnp.broadcast_to(leaf[s : s + 1], (HI * cols, cap)).astype(BF)
        w_ref[:, at] = jnp.where(position == leaf_of, moment_ref[:, at], zero)
    hi_of = [((iota((16, cap), 0) + 16 * i) // cols).astype(F32).astype(BF) for i in range(HI * cols // 16)]
    lo_of = [(iota((16, cap), 0) + 16 * i).astype(F32).astype(BF) for i in range(LO // 16)]

    def step(f):
        res = None
        for k in range(sources // 2):
            a = []
            b = []
            for s in (2 * k, 2 * k + 1):
                hi = hi_ref[pl.ds(s * feats + f, 16, stride=0), :].astype(BF)
                lo = lo_ref[pl.ds(s * feats + f, 16, stride=0), :].astype(BF)
                w = w_ref[:, s * cap : (s + 1) * cap]
                a.append(
                    jnp.concatenate(
                        [jnp.where(hi == of, w[i * 16 : (i + 1) * 16], zero) for i, of in enumerate(hi_of)], 0
                    )
                )
                b.append(jnp.concatenate([jnp.where(lo == of, one, zero) for of in lo_of], 0))
            part = lax.dot_general(
                jnp.concatenate(a, 1), jnp.concatenate(b, 1), NT, preferred_element_type=F32
            )
            res = part if res is None else res + part
        for half in range(2):
            parts = [res[h * cols : (h + 1) * cols] for h in (2 * half, 2 * half + 1)]
            halves[half][pl.ds(f, cols, stride=feats), :] = jnp.concatenate(parts, 1)

    def outputs(first):
        at = pl.ds(first, FINISH)
        return [
            pltpu.make_async_copy(source.at[:, at, :], target.at[:, at, :], sems.at[first // FINISH, i])
            for i, (source, target) in enumerate(
                ((leaf_ref, leaf_hbm), (child_ref, child_hbm), (node_ref, node_hbm))
            )
        ]

    for g in range(feats // FINISH):
        first = g * FINISH
        for f in range(first, first + FINISH):
            step(f)
        at = slice(first, first + FINISH)
        for half in range(2):
            lanes = slice(half * (BINS // 2), (half + 1) * (BINS // 2))
            value = [halves[half][c * feats + first : c * feats + first + FINISH, :] for c in range(cols)]
            for c in range(cols):
                leaf_ref[c, at, lanes] = value[c]
            pairs = [value[c] + value[c + 3] for c in (0, 1, 2, 6, 7, 8)]
            for c in range(6):
                child_ref[c, at, lanes] = pairs[c]
            for c in range(3):
                node_ref[c, at, lanes] = pairs[c] + pairs[c + 3]
        for copy in outputs(first):
            copy.start()
    for g in range(feats // FINISH):
        for copy in outputs(g * FINISH):
            copy.wait()


def specs(space, n):
    return [pl.BlockSpec(memory_space=space)] * n


def on_device(
    binned,
    node_index,
    treatment,
    outcome,
    unit_weight,
    root_feature,
    root_cutoff,
    child_feature,
    child_cutoff,
):
    rows, feats = binned.shape
    nodes = root_feature.shape[0]
    owners = lax.axis_size("rows")
    feat_devices = lax.axis_size("feat")
    cap = 2 * rows // nodes
    depth = feats + 8
    params = pltpu.CompilerParams(vmem_limit_bytes=24 << 20)
    in_hbm = lambda *xs: [pltpu.with_memory_space_constraint(x, pltpu.HBM) for x in xs]
    row = lambda dtype: pltpu.VMEM((1, rows), dtype)
    swap = lambda x, bit: lax.ppermute(x, "feat", [(i, i ^ bit) for i in range(feat_devices)])
    bins, node = in_hbm(binned.T, node_index.T)
    own, narrow = pl.pallas_call(
        decide_kernel,
        out_shape=[jax.ShapeDtypeStruct((8, rows), BF), jax.ShapeDtypeStruct((feats, rows), BF)],
        in_specs=specs(pltpu.SMEM, 1) + specs(pltpu.HBM, 6),
        out_specs=specs(pltpu.VMEM, 2),
        scratch_shapes=[
            row(jnp.int32),
            pltpu.VMEM((feats, rows), jnp.int32),
            pltpu.VMEM((1, nodes), jnp.int32),
            pltpu.VMEM((1, nodes), jnp.int32),
            pltpu.VMEM((1, 2 * nodes), jnp.int32),
            pltpu.VMEM((1, 2 * nodes), jnp.int32),
            pltpu.SemaphoreType.DMA((6,)),
        ],
        compiler_params=params,
        name="decide",
    )(
        lax.axis_index("feat").astype(jnp.int32)[None], node, bins,
        *in_hbm(root_feature[None], root_cutoff[None], child_feature[None], child_cutoff[None]),
    )
    other = swap(own, 1)
    buf, value = pl.pallas_call(
        place_kernel,
        out_shape=[
            jax.ShapeDtypeStruct((nodes, depth, cap), BF),
            jax.ShapeDtypeStruct((8, rows), F32),
        ],
        in_specs=specs(pltpu.VMEM, 1) + specs(pltpu.HBM, 4),
        out_specs=specs(pltpu.VMEM, 2),
        scratch_shapes=[
            row(jnp.int32), row(F32), row(F32), row(F32),
            pltpu.VMEM((nodes // 2 * feats, rows), BF),
            pltpu.SemaphoreType.DMA((4,)),
        ],
        compiler_params=params,
        name="place",
    )(narrow, node, *in_hbm(unit_weight[None], treatment[None], outcome[None]))
    buf = pl.pallas_call(
        value_kernel,
        out_shape=jax.ShapeDtypeStruct((nodes, depth, cap), BF),
        in_specs=specs(pltpu.VMEM, 3) + specs(pl.ANY, 1),
        out_specs=specs(pl.ANY, 1)[0],
        scratch_shapes=[pltpu.VMEM((nodes, 8, cap), BF), pltpu.SemaphoreType.DMA],
        input_output_aliases={3: 0},
        compiler_params=params,
        name="value",
    )(own, other, value, buf)
    got = lax.all_to_all(buf, "rows", 0, 0, tiled=True)
    half = pl.pallas_call(
        tail_kernel,
        out_shape=jax.ShapeDtypeStruct((3, owners, cap), BF),
        in_specs=specs(pltpu.VMEM, 1),
        out_specs=specs(pltpu.VMEM, 1)[0],
        compiler_params=params,
        name="tail",
    )(got)
    rest = swap(half, 3)
    digit = jax.ShapeDtypeStruct((owners * feats, cap), F32)
    hi, lo, moments = pl.pallas_call(
        prepare_kernel,
        out_shape=[digit, digit, jax.ShapeDtypeStruct((HI * 12, owners * cap), BF)],
        in_specs=specs(pltpu.VMEM, 1),
        out_specs=specs(pltpu.VMEM, 3),
        compiler_params=params,
        name="prepare",
    )(got)
    node_moments, child_moments, leaf_moments = pl.pallas_call(
        hist_kernel,
        out_shape=[jax.ShapeDtypeStruct((n * 3, feats, BINS), F32) for n in (1, 2, 4)],
        in_specs=specs(pltpu.VMEM, 5),
        out_specs=specs(pltpu.HBM, 3),
        scratch_shapes=[
            pltpu.VMEM((HI * 12, owners * cap), BF),
            pltpu.VMEM((12 * feats, BINS // 2), F32),
            pltpu.VMEM((12 * feats, BINS // 2), F32),
            pltpu.VMEM((3, feats, BINS), F32),
            pltpu.VMEM((6, feats, BINS), F32),
            pltpu.VMEM((12, feats, BINS), F32),
            pltpu.SemaphoreType.DMA((feats // FINISH, 3)),
        ],
        compiler_params=params,
        name="hist",
    )(hi, lo, moments, half, rest)
    return (
        node_moments.reshape(1, 3, feats, BINS),
        child_moments.reshape(2, 3, feats, BINS),
        leaf_moments.reshape(4, 3, feats, BINS),
    )


def solution(mesh):
    in_specs = (
        P("rows", "feat"),
        P("rows", None),
        P("rows"),
        P("rows"),
        P("rows"),
        P(),
        P(),
        P(),
        P(),
    )
    out_specs = (
        P("rows", None, "feat", None),
        P("rows", None, "feat", None),
        P("rows", None, "feat", None),
    )
    return jax.shard_map(
        on_device, mesh=mesh, in_specs=in_specs, out_specs=out_specs, check_vma=False
    )
```

```python
import jax
import jax.numpy as jnp
from jax import lax
from jax.experimental import pallas as pl
from jax.experimental.pallas import tpu as pltpu
from jax.sharding import PartitionSpec as P

BINS = 256
BF = jnp.bfloat16
F32 = jnp.float32
NT = (((1,), (1,)), ((), ()))
NN = (((1,), (0,)), ((), ()))
HI = 4
LO = BINS // HI
FINISH = 16


def iota(shape, axis):
    return lax.broadcasted_iota(jnp.int32, shape, axis)


def start_all(pairs, sems):
    copies = [pltpu.make_async_copy(pair[0], pair[1], sems.at[i]) for i, pair in enumerate(pairs)]
    for copy in copies:
        copy.start()
    return copies


def decide_kernel(
    place_ref, node_hbm, bins_hbm, rf_hbm, rc_hbm, cf_hbm, cc_hbm, bits_ref, out_ref, node_ref,
    bins_ref, rf_ref, rc_ref, cf_ref, cc_ref, sems,
):
    copies = start_all(
        (
            (node_hbm, node_ref), (rf_hbm, rf_ref), (rc_hbm, rc_ref), (cf_hbm, cf_ref),
            (cc_hbm, cc_ref), (bins_hbm, bins_ref),
        ),
        sems,
    )
    feats, rows = bins_ref.shape
    nodes = rf_ref.shape[1]
    first = place_ref[0] * feats
    for copy in copies[:5]:
        copy.wait()
    node = node_ref[...]

    def look_up(feature_row, cutoff_row, index, count):
        here = (feature_row - first == iota((feats, count), 0)).astype(F32)
        table = jnp.concatenate([here, jnp.broadcast_to(cutoff_row.astype(F32), (8, count))], 0)
        hot = (iota((count, rows), 0) == index).astype(F32).astype(BF)
        return lax.dot_general(table.astype(BF), hot, NN, preferred_element_type=F32)

    got = [
        look_up(rf_ref[...], rc_ref[...], node, nodes),
        look_up(cf_ref[...], cc_ref[...], 2 * node, 2 * nodes),
        look_up(cf_ref[...], cc_ref[...], 2 * node + 1, 2 * nodes),
    ]
    copies[5].wait()
    bins = bins_ref[...].astype(F32)
    out_ref[...] = bins.astype(BF)
    bits = [
        jnp.sum(jnp.where(bins > g[feats : feats + 1], g[:feats], 0.0), 0, keepdims=True) for g in got
    ]
    bits_ref[...] = jnp.concatenate(bits + [jnp.zeros((5, rows), F32)], 0).astype(BF)


def place_kernel(
    bins_ref, node_ref, w_hbm, t_hbm, y_hbm, out_ref, value_ref, hot_ref, w_ref, t_ref, y_ref, a_ref,
    sems,
):
    copies = start_all(((w_hbm, w_ref), (t_hbm, t_ref), (y_hbm, y_ref)), sems)
    feats, rows = bins_ref.shape
    nodes, depth, cap = out_ref.shape
    blocks = rows // 256
    node = node_ref[...]
    hot = (iota((nodes, rows), 0) == node).astype(F32)
    stacked = jnp.concatenate([hot[:, b * 256 : (b + 1) * 256] for b in range(blocks)], 0)
    before = (iota((256, 256), 0) < iota((256, 256), 1)).astype(F32).astype(BF)
    ones = jnp.ones((256, 256), BF)
    inner = lax.dot_general(stacked.astype(BF), before, NN, preferred_element_type=F32)
    total = lax.dot_general(stacked.astype(BF), ones, NN, preferred_element_type=F32)
    carry = jnp.zeros((nodes, 256), F32)
    ranks = []
    for b in range(blocks):
        part = slice(b * nodes, (b + 1) * nodes)
        ranks.append(jnp.sum(stacked[part] * (inner[part] + carry), 0, keepdims=True))
        carry = carry + total[part]
    rank = jnp.concatenate(ranks, 1)
    code = rank.astype(jnp.int32) + node % 2 * cap
    slot_hot = (iota((2 * cap, rows), 0) == code).astype(F32).astype(BF)
    hot_ref[...] = slot_hot
    bins = bins_ref[...]
    pair = jnp.broadcast_to(node // 2, (feats, rows))
    for p in range(nodes // 2):
        a_ref[p * feats : (p + 1) * feats, :] = jnp.where(pair == p, bins, jnp.zeros((), BF))
    moved = lax.dot_general(a_ref[...], slot_hot, NT, preferred_element_type=F32).astype(BF)
    for p in range(nodes // 2):
        piece = moved[p * feats : (p + 1) * feats]
        out_ref[2 * p, :feats, :] = piece[:, :cap]
        out_ref[2 * p + 1, :feats, :] = piece[:, cap:]
    for copy in copies:
        copy.wait()
    w = w_ref[...]
    t = t_ref[...]
    y = y_ref[...]
    value_ref[...] = jnp.concatenate(
        [w, w * t * t, w * t * y, (node // 2).astype(F32), jnp.zeros((4, rows), F32)], 0
    )


def value_kernel(bits_ref, other_ref, value_ref, hot_ref, buf_ref, out_ref, part_ref, sem):
    nodes, _, cap = part_ref.shape
    rows = value_ref.shape[1]
    bits = bits_ref[...].astype(F32) + other_ref[...].astype(F32)
    carried = jnp.concatenate([value_ref[:3, :], bits[:5]], 0)
    pair = jnp.broadcast_to(value_ref[3:4, :], (8, rows))
    spread = jnp.concatenate(
        [jnp.where(pair == float(p), carried, 0.0) for p in range(nodes // 2)], 0
    ).astype(BF)
    moved = lax.dot_general(spread, hot_ref[...], NT, preferred_element_type=F32).astype(BF)
    for p in range(nodes // 2):
        piece = moved[p * 8 : (p + 1) * 8]
        part_ref[2 * p] = piece[:, :cap]
        part_ref[2 * p + 1] = piece[:, cap:]
    copy = pltpu.make_async_copy(part_ref, out_ref.at[:, pl.ds(out_ref.shape[1] - 8, 8), :], sem)
    copy.start()
    copy.wait()


def tail_kernel(got_ref, bits_ref):
    sources, depth, _ = got_ref.shape
    tails = [got_ref[s, depth - 8 :, :].astype(F32) for s in range(sources)]
    for k in range(3):
        bits_ref[k] = jnp.concatenate([tail[3 + k : 4 + k] for tail in tails], 0).astype(BF)


def prepare_kernel(got_ref, hi_ref, lo_ref, moment_ref):
    sources, depth, cap = got_ref.shape
    feats = depth - 8
    which = iota((moment_ref.shape[0], cap), 0) % 3
    for s in range(sources):
        x = got_ref[s, :feats, :].astype(F32)
        hi = jnp.floor(x * (1.0 / LO))
        hi_ref[s * feats : (s + 1) * feats, :] = hi
        lo_ref[s * feats : (s + 1) * feats, :] = x - hi * LO
        tail = got_ref[s, feats:, :].astype(F32)
        moments = jnp.where(which == 0, tail[0:1], jnp.where(which == 1, tail[1:2], tail[2:3]))
        moment_ref[:, s * cap : (s + 1) * cap] = moments.astype(BF)


def hist_kernel(
    hi_ref, lo_ref, moment_ref, bits_ref, other_ref, node_hbm, child_hbm, leaf_hbm, w_ref, half0_ref,
    half1_ref, node_ref, child_ref, leaf_ref, sems,
):
    cols, feats, _ = leaf_ref.shape
    _, sources, cap = bits_ref.shape
    halves = (half0_ref, half1_ref)
    one = jnp.ones((), BF)
    zero = jnp.zeros((), BF)
    bits = bits_ref[...].astype(F32) + other_ref[...].astype(F32)
    leaf = 2.0 * bits[0] + jnp.where(bits[0] > 0.5, bits[2], bits[1])
    leaf_of = (iota((HI * cols, cap), 0) % cols // 3).astype(F32).astype(BF)
    for s in range(sources):
        at = slice(s * cap, (s + 1) * cap)
        position = jnp.broadcast_to(leaf[s : s + 1], (HI * cols, cap)).astype(BF)
        w_ref[:, at] = jnp.where(position == leaf_of, moment_ref[:, at], zero)
    hi_of = [((iota((16, cap), 0) + 16 * i) // cols).astype(F32).astype(BF) for i in range(HI * cols // 16)]
    lo_of = [(iota((16, cap), 0) + 16 * i).astype(F32).astype(BF) for i in range(LO // 16)]

    def step(f):
        res = None
        for k in range(sources // 2):
            a = []
            b = []
            for s in (2 * k, 2 * k + 1):
                hi = hi_ref[pl.ds(s * feats + f, 16, stride=0), :].astype(BF)
                lo = lo_ref[pl.ds(s * feats + f, 16, stride=0), :].astype(BF)
                w = w_ref[:, s * cap : (s + 1) * cap]
                a.append(
                    jnp.concatenate(
                        [jnp.where(hi == of, w[i * 16 : (i + 1) * 16], zero) for i, of in enumerate(hi_of)], 0
                    )
                )
                b.append(jnp.concatenate([jnp.where(lo == of, one, zero) for of in lo_of], 0))
            part = lax.dot_general(
                jnp.concatenate(a, 1), jnp.concatenate(b, 1), NT, preferred_element_type=F32
            )
            res = part if res is None else res + part
        for half in range(2):
            parts = [res[h * cols : (h + 1) * cols] for h in (2 * half, 2 * half + 1)]
            halves[half][pl.ds(f, cols, stride=feats), :] = jnp.concatenate(parts, 1)

    def outputs(first):
        at = pl.ds(first, FINISH)
        return [
            pltpu.make_async_copy(source.at[:, at, :], target.at[:, at, :], sems.at[first // FINISH, i])
            for i, (source, target) in enumerate(
                ((leaf_ref, leaf_hbm), (child_ref, child_hbm), (node_ref, node_hbm))
            )
        ]

    for g in range(feats // FINISH):
        first = g * FINISH
        for f in range(first, first + FINISH):
            step(f)
        at = slice(first, first + FINISH)
        for half in range(2):
            lanes = slice(half * (BINS // 2), (half + 1) * (BINS // 2))
            value = [halves[half][c * feats + first : c * feats + first + FINISH, :] for c in range(cols)]
            for c in range(cols):
                leaf_ref[c, at, lanes] = value[c]
            pairs = [value[c] + value[c + 3] for c in (0, 1, 2, 6, 7, 8)]
            for c in range(6):
                child_ref[c, at, lanes] = pairs[c]
            for c in range(3):
                node_ref[c, at, lanes] = pairs[c] + pairs[c + 3]
        for copy in outputs(first):
            copy.start()
    for g in range(feats // FINISH):
        for copy in outputs(g * FINISH):
            copy.wait()


def specs(space, n):
    return [pl.BlockSpec(memory_space=space)] * n


def on_device(
    binned,
    node_index,
    treatment,
    outcome,
    unit_weight,
    root_feature,
    root_cutoff,
    child_feature,
    child_cutoff,
):
    rows, feats = binned.shape
    nodes = root_feature.shape[0]
    owners = lax.axis_size("rows")
    feat_devices = lax.axis_size("feat")
    cap = 2 * rows // nodes
    depth = feats + 8
    params = pltpu.CompilerParams(vmem_limit_bytes=24 << 20)
    in_hbm = lambda *xs: [pltpu.with_memory_space_constraint(x, pltpu.HBM) for x in xs]
    row = lambda dtype: pltpu.VMEM((1, rows), dtype)
    swap = lambda x, bit: lax.ppermute(x, "feat", [(i, i ^ bit) for i in range(feat_devices)])
    bins, node = in_hbm(binned.T, node_index.T)
    own, narrow, kept = pl.pallas_call(
        decide_kernel,
        out_shape=[
            jax.ShapeDtypeStruct((8, rows), BF),
            jax.ShapeDtypeStruct((feats, rows), BF),
            jax.ShapeDtypeStruct((1, rows), jnp.int32),
        ],
        in_specs=specs(pltpu.SMEM, 1) + specs(pltpu.HBM, 6),
        out_specs=specs(pltpu.VMEM, 3),
        scratch_shapes=[
            pltpu.VMEM((feats, rows), jnp.int32),
            pltpu.VMEM((1, nodes), jnp.int32),
            pltpu.VMEM((1, nodes), jnp.int32),
            pltpu.VMEM((1, 2 * nodes), jnp.int32),
            pltpu.VMEM((1, 2 * nodes), jnp.int32),
            pltpu.SemaphoreType.DMA((6,)),
        ],
        compiler_params=params,
        name="decide",
    )(
        lax.axis_index("feat").astype(jnp.int32)[None], node, bins,
        *in_hbm(root_feature[None], root_cutoff[None], child_feature[None], child_cutoff[None]),
    )
    other = swap(own, 2)
    buf, value, slot_hot = pl.pallas_call(
        place_kernel,
        out_shape=[
            jax.ShapeDtypeStruct((nodes, depth, cap), BF),
            jax.ShapeDtypeStruct((8, rows), F32),
            jax.ShapeDtypeStruct((2 * cap, rows), BF),
        ],
        in_specs=specs(pltpu.VMEM, 2) + specs(pltpu.HBM, 3),
        out_specs=specs(pltpu.VMEM, 3),
        scratch_shapes=[
            row(F32), row(F32), row(F32),
            pltpu.VMEM((nodes // 2 * feats, rows), BF),
            pltpu.SemaphoreType.DMA((3,)),
        ],
        compiler_params=params,
        name="place",
    )(narrow, kept, *in_hbm(unit_weight[None], treatment[None], outcome[None]))
    buf = pl.pallas_call(
        value_kernel,
        out_shape=jax.ShapeDtypeStruct((nodes, depth, cap), BF),
        in_specs=specs(pltpu.VMEM, 4) + specs(pl.ANY, 1),
        out_specs=specs(pl.ANY, 1)[0],
        scratch_shapes=[pltpu.VMEM((nodes, 8, cap), BF), pltpu.SemaphoreType.DMA],
        input_output_aliases={4: 0},
        compiler_params=params,
        name="value",
    )(own, other, value, slot_hot, buf)
    got = lax.all_to_all(buf, "rows", 0, 0, tiled=True)
    half = pl.pallas_call(
        tail_kernel,
        out_shape=jax.ShapeDtypeStruct((3, owners, cap), BF),
        in_specs=specs(pltpu.VMEM, 1),
        out_specs=specs(pltpu.VMEM, 1)[0],
        compiler_params=params,
        name="tail",
    )(got)
    rest = swap(half, 1)
    digit = jax.ShapeDtypeStruct((owners * feats, cap), F32)
    hi, lo, moments = pl.pallas_call(
        prepare_kernel,
        out_shape=[digit, digit, jax.ShapeDtypeStruct((HI * 12, owners * cap), BF)],
        in_specs=specs(pltpu.VMEM, 1),
        out_specs=specs(pltpu.VMEM, 3),
        compiler_params=params,
        name="prepare",
    )(got)
    node_moments, child_moments, leaf_moments = pl.pallas_call(
        hist_kernel,
        out_shape=[jax.ShapeDtypeStruct((n * 3, feats, BINS), F32) for n in (1, 2, 4)],
        in_specs=specs(pltpu.VMEM, 5),
        out_specs=specs(pltpu.HBM, 3),
        scratch_shapes=[
            pltpu.VMEM((HI * 12, owners * cap), BF),
            pltpu.VMEM((12 * feats, BINS // 2), F32),
            pltpu.VMEM((12 * feats, BINS // 2), F32),
            pltpu.VMEM((3, feats, BINS), F32),
            pltpu.VMEM((6, feats, BINS), F32),
            pltpu.VMEM((12, feats, BINS), F32),
            pltpu.SemaphoreType.DMA((feats // FINISH, 3)),
        ],
        compiler_params=params,
        name="hist",
    )(hi, lo, moments, half, rest)
    return (
        node_moments.reshape(1, 3, feats, BINS),
        child_moments.reshape(2, 3, feats, BINS),
        leaf_moments.reshape(4, 3, feats, BINS),
    )


def solution(mesh):
    in_specs = (
        P("rows", "feat"),
        P("rows", None),
        P("rows"),
        P("rows"),
        P("rows"),
        P(),
        P(),
        P(),
        P(),
    )
    out_specs = (
        P("rows", None, "feat", None),
        P("rows", None, "feat", None),
        P("rows", None, "feat", None),
    )
    return jax.shard_map(
        on_device, mesh=mesh, in_specs=in_specs, out_specs=out_specs, check_vma=False
    )
```
